256 devices in a mesh: segment: 8 (over y, z_lo), frame: 32 (over x, z_hi, core).
Axes of the slice: x: 4, y: 4, z: 8 (z_hi: 4, z_lo: 2; z = z_hi * 2 + z_lo), core: 2. Of those that a mesh axis runs over, the one named last changes fastest.
Arguments:
- noisy_clips: bfloat16 [4, 32, 16, 16, 512], P(None, 'frame'), may hold values from -6 to 6
- conv_first: bfloat16 [8, 9, 512, 512], P('segment', None, 'frame'), may hold values from -0.09375 to 0.09375
- conv_second: bfloat16 [8, 9, 512, 512], P('segment', None, 'frame'), may hold values from -0.09375 to 0.09375
- temporal: bfloat16 [8, 3, 512, 512], P('segment', None, 'frame'), may hold values from -0.15625 to 0.15625
Outputs:
- denoised: bfloat16 [4, 32, 16, 16, 512], P(None, 'frame', 'segment')
The draws below stay inside these ranges and needn't reach their ends.
All inputs are finite; a program needn't handle non-finite values.
Results may differ from the reference program's by a relative error of at most 0.013.
Values may be sent and summed in bfloat16 or wider, within the bound.
No kernel may reach another device: no remote copies, remote signals or barrier semaphores. Data moves between devices by JAX's collectives and lax.ppermute only.
A program may use at most 64 MiB of HBM per device.

```python
import jax
import jax.numpy as jnp

C = 512
MAP = 16
CLIPS = 4
SECTIONS = 8
FRAMES = 32


def shard_levels(stream_key, shape, split, low, high):
    factor_of = 1.0
    for position, blocks in split:
        steps = jax.random.uniform(jax.random.fold_in(jax.random.fold_in(stream_key, 6), position), (blocks,), jnp.float32, low / len(split), high / len(split))
        factor_of = factor_of * jnp.repeat(jnp.exp(steps), shape[position] // blocks).reshape((-1,) + (1,) * (len(shape) - 1 - position))
    return factor_of


def gaussian(own_key, shape, scale, reach, shards=(), kind=jnp.bfloat16):
    array = scale * jax.random.normal(own_key, shape, jnp.float32)
    if shards:
        array = array * shard_levels(own_key, shape, shards, -0.22, 0.18)
    return jnp.clip(array, -reach, reach).astype(kind)


def setup_inputs(seed: int = 0) -> dict:
    key_list = jax.random.split(jax.random.key(seed), 5)
    return {
        "noisy_clips": gaussian(key_list[0], (CLIPS, FRAMES, MAP, MAP, C), 1.0, 6.0, ((1, 32),)),
        "conv_first": gaussian(key_list[1], (SECTIONS, 9, C, C), (9 * C) ** -0.5, 0.09375, ((0, 8), (2, 32))),
        "conv_second": gaussian(key_list[2], (SECTIONS, 9, C, C), (9 * C) ** -0.5, 0.09375, ((0, 8), (2, 32))),
        "temporal": gaussian(key_list[3], (SECTIONS, 3, C, C), (3 * C) ** -0.5, 0.15625, ((0, 8), (2, 32))),
    }


skip_scale = 0.7071067811865476


def spatial(field_in, kernel):
    extent = field_in.shape[1]
    channels = field_in.shape[3]
    padded = jnp.pad(field_in, ((0, 0), (1, 1), (1, 1), (0, 0)))
    accumulated = jnp.zeros((field_in.shape[0] * extent * extent, channels), jnp.float32)
    for row_shift in range(3):
        for col_shift in range(3):
            window = padded[:, row_shift:row_shift + extent, col_shift:col_shift + extent, :].reshape(-1, channels)
            accumulated = accumulated + jnp.dot(window, kernel[3 * row_shift + col_shift], preferred_element_type=jnp.float32)
    return accumulated.reshape(field_in.shape)


def section(entering, first_kernel, second_kernel, time_kernel):
    full_shape = entering.shape
    channels = full_shape[4]
    frame_total = full_shape[1]
    flat = entering.reshape((-1,) + full_shape[2:])
    activated = jax.nn.silu(spatial(flat, first_kernel)).astype(jnp.bfloat16)
    spatial_term = spatial(activated, second_kernel).reshape(full_shape)
    activated = activated.reshape(full_shape)
    extended = jnp.pad(activated, ((0, 0), (1, 1), (0, 0), (0, 0), (0, 0)))
    time_term = jnp.zeros(full_shape, jnp.float32)
    for offset in range(3):
        window = extended[:, offset:offset + frame_total].reshape(-1, channels)
        time_term = time_term + jnp.dot(window, time_kernel[offset], preferred_element_type=jnp.float32).reshape(full_shape)
    return (entering.astype(jnp.float32) + jax.nn.silu(spatial_term + time_term)).astype(jnp.bfloat16)


def reference(noisy_clips, conv_first, conv_second, temporal):
    sections = conv_first.shape[0]
    half_sections = sections // 2
    current = noisy_clips
    inputs_down = []
    for section_index in range(sections):
        if section_index < half_sections:
            entering = current
            inputs_down.append(current)
        else:
            partner = inputs_down[sections - 1 - section_index]
            entering = ((current.astype(jnp.float32) + partner.astype(jnp.float32)) * skip_scale).astype(jnp.bfloat16)
        current = section(entering, conv_first[section_index], conv_second[section_index], temporal[section_index])
    return current
```

```python
import itertools

import jax
import jax.numpy as jnp
from jax import lax
from jax.experimental import pallas as pl
from jax.experimental.pallas import tpu as pltpu
from jax.sharding import Mesh
from jax.sharding import PartitionSpec as P

skip_scale = 0.7071067811865476
AXES = ("y", "zlo", "x", "zhi", "core")
SEGMENT = ("y", "zlo")
FRAME = ("x", "zhi", "core")
PLANE = ("zlo", "x", "zhi", "core")
NY, NX, NZ = 4, 4, 8
SIDE = 16
CH = 512
PIX = SIDE * SIDE
F32 = jnp.float32
BF16 = jnp.bfloat16


def flat(x, y, z, core):
    return (((y * 2 + z % 2) * 4 + x) * 4 + z // 2) * 2 + core


def sent(value, route):
    pairs = []
    for x, y, z, core in itertools.product(range(NX), range(NY), range(NZ), range(2)):
        target = route(x, y, z, core)
        if target is not None:
            pairs.append((flat(x, y, z, core), flat(*target)))
    return lax.ppermute(value, AXES, pairs)


def to_right(x, y, z, core):
    q = 2 * z + core + 1
    return (x, y, q // 2, q % 2) if q < 2 * NZ else None


def to_left(x, y, z, core):
    q = 2 * z + core - 1
    return (x, y, q // 2, q % 2) if q >= 0 else None


def plane_to_plane(source, target):
    return lambda x, y, z, core: (x, target, z, core) if y == source else None


def silu(u):
    return u / (1.0 + jnp.exp(-u))


def widen(frame, wide_ref, index):
    full = frame.astype(F32)
    column = lax.broadcasted_iota(jnp.int32, (PIX, CH), 0) % SIDE
    before = jnp.where(column == 0, 0.0, pltpu.roll(full, 1, 0)).astype(BF16)
    after = jnp.where(column == SIDE - 1, 0.0, pltpu.roll(full, PIX - 1, 0)).astype(BF16)
    edge = jnp.zeros((SIDE, 3 * CH), BF16)
    wide_ref[index, 0:SIDE, :] = edge
    wide_ref[index, SIDE + PIX : 2 * SIDE + PIX, :] = edge
    wide_ref[index, SIDE : SIDE + PIX, 0:CH] = before
    wide_ref[index, SIDE : SIDE + PIX, CH : 2 * CH] = frame
    wide_ref[index, SIDE : SIDE + PIX, 2 * CH : 3 * CH] = after


def conv_rows(wide_ref, weights, index, dy):
    rows = wide_ref[index, pl.ds(pl.multiple_of(dy * SIDE, SIDE), PIX), :]
    return jnp.dot(rows, weights, preferred_element_type=F32)


def first_kernel(e_ref, w_ref, out_ref, wide_ref, acc_ref):
    dy = pl.program_id(0)
    frames = e_ref.shape[0]

    @pl.when(dy == 0)
    def _():
        for i in range(frames):
            widen(e_ref[i], wide_ref, i)

    weights = w_ref[...].reshape(3 * CH, CH)
    for i in range(frames):
        part = conv_rows(wide_ref, weights, i, dy)

        @pl.when(dy == 0)
        def _():
            acc_ref[i] = part

        @pl.when(dy == 1)
        def _():
            acc_ref[i] += part

        @pl.when(dy == 2)
        def _():
            out_ref[i] = silu(acc_ref[i] + part).astype(BF16)


def second_kernel(a_ref, w_ref, acc_ref, wide_ref):
    step = pl.program_id(0)
    frames = a_ref.shape[0]

    @pl.when(step == 0)
    def _():
        for i in range(frames):
            widen(a_ref[i], wide_ref, i)

    @pl.when(step < 3)
    def _():
        weights = w_ref[...].reshape(3 * CH, CH)
        for i in range(frames):
            part = conv_rows(wide_ref, weights, i, step)

            @pl.when(step == 0)
            def _():
                acc_ref[i] = part

            @pl.when(step > 0)
            def _():
                acc_ref[i] += part

    @pl.when(step == 3)
    def _():
        for i in range(frames):
            total = acc_ref[i]
            for j in range(max(0, i - 1), min(frames, i + 2)):
                total += jnp.dot(a_ref[j], w_ref[j - i + 1], preferred_element_type=F32)
            acc_ref[i] = total


def last_kernel(acc_ref, e_ref, left_ref, right_ref, w_ref, out_ref):
    last = e_ref.shape[0] - 1
    for i in range(last + 1):
        total = acc_ref[i]
        if i == 0:
            total += jnp.dot(left_ref[...], w_ref[0], preferred_element_type=F32)
        if i == last:
            total += jnp.dot(right_ref[...], w_ref[2], preferred_element_type=F32)
        out_ref[i] = (e_ref[i].astype(F32) + silu(total)).astype(BF16)


def whole(*shape):
    return pl.BlockSpec(shape, lambda *_: (0,) * len(shape))


def params(mib):
    return pltpu.CompilerParams(vmem_limit_bytes=mib << 20)


def cost(taps, weight_taps):
    return pl.CostEstimate(
        flops=2 * taps * PIX * CH * CH,
        bytes_accessed=weight_taps * CH * CH * 2 + 4 * PIX * CH * 2,
        transcendentals=2 * PIX * CH,
    )


def section(e, first, second, which):
    frames = e.shape[0]
    activated = pl.pallas_call(
        first_kernel,
        grid=(3,),
        in_specs=[
            whole(frames, PIX, CH),
            pl.BlockSpec((3, CH, CH), lambda i: (i, which, 0)),
        ],
        out_specs=whole(frames, PIX, CH),
        out_shape=jax.ShapeDtypeStruct((frames, PIX, CH), BF16),
        scratch_shapes=[
            pltpu.VMEM((frames, PIX + 2 * SIDE, 3 * CH), BF16),
            pltpu.VMEM((frames, PIX, CH), F32),
        ],
        compiler_params=params(20),
        cost_estimate=cost(9 * frames, 9),
        name="conv_first",
    )(e, first)
    left = sent(activated[frames - 1], to_right)
    right = sent(activated[0], to_left)
    acc = pl.pallas_call(
        second_kernel,
        grid=(4,),
        in_specs=[
            whole(frames, PIX, CH),
            pl.BlockSpec((3, CH, CH), lambda i: (i, which, 0)),
        ],
        out_specs=whole(frames, PIX, CH),
        out_shape=jax.ShapeDtypeStruct((frames, PIX, CH), F32),
        scratch_shapes=[pltpu.VMEM((frames, PIX + 2 * SIDE, 3 * CH), BF16)],
        compiler_params=params(20),
        cost_estimate=cost(11 * frames, 12),
        name="conv_second",
    )(activated, second)
    return pl.pallas_call(
        last_kernel,
        grid=(1,),
        in_specs=[
            whole(frames, PIX, CH),
            whole(frames, PIX, CH),
            whole(PIX, CH),
            whole(PIX, CH),
            pl.BlockSpec((3, CH, CH), lambda i: (3, which, 0)),
        ],
        out_specs=whole(frames, PIX, CH),
        out_shape=jax.ShapeDtypeStruct((frames, PIX, CH), BF16),
        compiler_params=params(20),
        cost_estimate=cost(2, 3),
        name="halo_and_residual",
    )(acc, e, left, right, second)


def joined(h, skip):
    return ((h.astype(F32) + skip.astype(F32)) * skip_scale).astype(BF16)


def spread_clips(noisy):
    zlo, core, x = lax.axis_index("zlo"), lax.axis_index("core"), lax.axis_index("x")
    clips = noisy.reshape(4, PIX, CH)
    got = []
    for r in range(2):
        clip = lax.dynamic_index_in_dim(clips, 2 * zlo + (r ^ core), 0, keepdims=False)

        def route(sx, sy, sz, sc, r=r):
            hi, lo = sz // 2, sz % 2
            return (2 * lo + (r ^ sc), sy, 2 * sx + hi // 2, hi % 2)

        got.append(sent(clip, route))
    even = x % 2 == 0
    return jnp.stack([jnp.where(even, got[0], got[1]), jnp.where(even, got[1], got[0])])


def deliver(h):
    y, zlo, core, x = (lax.axis_index(n) for n in ("y", "zlo", "core", "x"))
    rows = h.reshape(2, NY, 2, 2, SIDE, CH)
    mine = rows[:, NY - 1]
    for target in range(NY - 1):
        got = sent(rows[:, target], plane_to_plane(NY - 1, target))
        mine = jnp.where(y == target, got, mine)
    messages = mine.reshape(4, 2, SIDE, CH)
    slots = []
    for r in range(4):
        message = lax.dynamic_index_in_dim(messages, x ^ r, 0, keepdims=False)

        def route(sx, sy, sz, sc, r=r):
            k, lo = (sx ^ r) // 2, (sx ^ r) % 2
            return (sz // 2, sy, 2 * (2 * (sz % 2) + sc) + lo, k)

        slots.append(sent(message, route))
    slots = jnp.stack(slots)
    here = core * 2 + zlo
    out = [lax.dynamic_index_in_dim(slots, here ^ c, 0, keepdims=False) for c in range(4)]
    return jnp.stack(out)[:, None]


def on_device(noisy, conv_first, conv_second, temporal):
    first = lax.all_gather(conv_first[0], PLANE, axis=1, tiled=True)
    tail = jnp.concatenate([conv_second[0], temporal[0]], axis=0)
    second = lax.all_gather(tail, PLANE, axis=1, tiled=True)
    e0 = spread_clips(noisy)
    e1 = section(e0, first, second, 0)
    skip6 = sent(e1, plane_to_plane(0, 3))
    h = section(e1, first, second, 1)
    e2 = sent(h, plane_to_plane(0, 1))
    skip5 = sent(e2, plane_to_plane(1, 2))
    e3 = section(e2, first, second, 0)
    h = section(e3, first, second, 1)
    e4 = sent(joined(h, e3), plane_to_plane(1, 2))
    h = section(e4, first, second, 0)
    h = section(joined(h, skip5), first, second, 1)
    h = sent(h, plane_to_plane(2, 3))
    h = section(joined(h, skip6), first, second, 0)
    h = section(joined(h, e0), first, second, 1)
    return deliver(h)


def solution(mesh):
    fine = Mesh(mesh.devices.reshape(NY, 2, NX, NZ // 2, 2), AXES)
    weight_spec = P(SEGMENT, None, FRAME, None)
    return jax.shard_map(
        on_device,
        mesh=fine,
        in_specs=(P(None, FRAME), weight_spec, weight_spec, weight_spec),
        out_specs=P(None, FRAME, SEGMENT),
        check_vma=False,
    )
```

```python
import itertools

import jax
import jax.numpy as jnp
import numpy as np
from jax import lax
from jax.experimental import pallas as pl
from jax.experimental.pallas import tpu as pltpu
from jax.sharding import Mesh
from jax.sharding import PartitionSpec as P

skip_scale = 0.7071067811865476
AXES = ("y", "zlo", "x", "zhi", "core")
SEGMENT = ("y", "zlo")
FRAME = ("x", "zhi", "core")
PLANE = ("zlo", "x", "zhi", "core")
NY, NX, NZ = 4, 4, 8
SIDE = 16
CH = 512
PIX = SIDE * SIDE
F32 = jnp.float32
BF16 = jnp.bfloat16


def flat(x, y, z, core):
    return (((y * 2 + z % 2) * 4 + x) * 4 + z // 2) * 2 + core


def sent(value, route):
    pairs = []
    for x, y, z, core in itertools.product(range(NX), range(NY), range(NZ), range(2)):
        target = route(x, y, z, core)
        if target is not None:
            pairs.append((flat(x, y, z, core), flat(*target)))
    return lax.ppermute(value, AXES, pairs)


def to_right(x, y, z, core):
    q = 2 * z + core + 1
    return (x, y, q // 2, q % 2) if q < 2 * NZ else None


def to_left(x, y, z, core):
    q = 2 * z + core - 1
    return (x, y, q // 2, q % 2) if q >= 0 else None


def along(dx, dz):
    return lambda x, y, z, core: ((x + dx) % NX, y, (z + dz) % NZ, core)


def other_core(x, y, z, core):
    return (x, y, z, 1 - core)


def plane_to_plane(source, target):
    return lambda x, y, z, core: (x, target, z, core) if y == source else None


def silu(u):
    return u / (1.0 + jnp.exp(-u))


def widen(frame, wide_ref, index):
    full = frame.astype(F32)
    column = lax.broadcasted_iota(jnp.int32, (PIX, CH), 0) % SIDE
    before = jnp.where(column == 0, 0.0, pltpu.roll(full, 1, 0)).astype(BF16)
    after = jnp.where(column == SIDE - 1, 0.0, pltpu.roll(full, PIX - 1, 0)).astype(BF16)
    edge = jnp.zeros((SIDE, 3 * CH), BF16)
    wide_ref[index, 0:SIDE, :] = edge
    wide_ref[index, SIDE + PIX : 2 * SIDE + PIX, :] = edge
    wide_ref[index, SIDE : SIDE + PIX, 0:CH] = before
    wide_ref[index, SIDE : SIDE + PIX, CH : 2 * CH] = frame
    wide_ref[index, SIDE : SIDE + PIX, 2 * CH : 3 * CH] = after


def conv_rows(wide_ref, weights, index, dy):
    rows = wide_ref[index, pl.ds(pl.multiple_of(dy * SIDE, SIDE), PIX), :]
    return jnp.dot(rows, weights, preferred_element_type=F32)


def first_kernel(e_ref, w_ref, out_ref, wide_ref, acc_ref):
    dy = pl.program_id(0)
    frames = e_ref.shape[0]

    @pl.when(dy == 0)
    def _():
        for i in range(frames):
            widen(e_ref[i], wide_ref, i)

    weights = w_ref[...].reshape(3 * CH, CH)

    @pl.loop(0, frames)
    def _(i):
        part = conv_rows(wide_ref, weights, i, dy)

        @pl.when(dy == 0)
        def _():
            acc_ref[i] = part

        @pl.when(dy == 1)
        def _():
            acc_ref[i] += part

        @pl.when(dy == 2)
        def _():
            out_ref[i] = silu(acc_ref[i] + part).astype(BF16)


def second_kernel(a_ref, w_ref, acc_ref, wide_ref):
    step = pl.program_id(0)
    frames = a_ref.shape[0]

    @pl.when(step == 0)
    def _():
        for i in range(frames):
            widen(a_ref[i], wide_ref, i)

    @pl.when(step < 3)
    def _():
        weights = stacked_taps(w_ref, range(3))

        @pl.loop(0, frames)
        def _(i):
            part = conv_rows(wide_ref, weights, i, step)

            @pl.when(step == 0)
            def _():
                acc_ref[i] = part

            @pl.when(step > 0)
            def _():
                acc_ref[i] += part

    @pl.when(step == 3)
    def _():
        for i in range(frames):
            total = acc_ref[i]
            for j in range(max(0, i - 1), min(frames, i + 2)):
                total += jnp.dot(a_ref[j], stacked_taps(w_ref, [j - i + 1]), preferred_element_type=F32)
            acc_ref[i] = total


def last_kernel(acc_ref, e_ref, left_ref, right_ref, w_ref, out_ref):
    last = e_ref.shape[0] - 1
    for i in range(last + 1):
        total = acc_ref[i]
        if i == 0:
            total += jnp.dot(left_ref[...], stacked_taps(w_ref, [0]), preferred_element_type=F32)
        if i == last:
            total += jnp.dot(right_ref[...], stacked_taps(w_ref, [2]), preferred_element_type=F32)
        out_ref[i] = (e_ref[i].astype(F32) + silu(total)).astype(BF16)


def whole(*shape):
    return pl.BlockSpec(shape, lambda *_: (0,) * len(shape))


def tail_block(which, tap_block):
    shape = (NX, 2, 3, None, NZ // 2, SIDE, CH)
    return pl.BlockSpec(shape, lambda i: (0, 0, tap_block(i), which, 0, 0, 0))


def params(mib):
    return pltpu.CompilerParams(vmem_limit_bytes=mib << 20)


def cost(taps, weight_taps):
    return pl.CostEstimate(
        flops=2 * taps * PIX * CH * CH,
        bytes_accessed=weight_taps * CH * CH * 2 + 4 * PIX * CH * 2,
        transcendentals=2 * PIX * CH,
    )


def stacked_taps(w_ref, taps):
    order = itertools.product(taps, range(NX), range(NZ // 2), range(2))
    return jnp.concatenate([w_ref[x, core, t, hi] for t, x, hi, core in order], axis=0)


def section(e, first, second, which):
    frames = e.shape[0]
    activated = pl.pallas_call(
        first_kernel,
        grid=(3,),
        in_specs=[
            whole(frames, PIX, CH),
            pl.BlockSpec((3, CH, CH), lambda i: (i, which, 0)),
        ],
        out_specs=whole(frames, PIX, CH),
        out_shape=jax.ShapeDtypeStruct((frames, PIX, CH), BF16),
        scratch_shapes=[
            pltpu.VMEM((frames, PIX + 2 * SIDE, 3 * CH), BF16),
            pltpu.VMEM((frames, PIX, CH), F32),
        ],
        compiler_params=params(20),
        cost_estimate=cost(9 * frames, 9),
        name="conv_first",
    )(e, first)
    left = sent(activated[frames - 1], to_right)
    right = sent(activated[0], to_left)
    acc = pl.pallas_call(
        second_kernel,
        grid=(4,),
        in_specs=[
            whole(frames, PIX, CH),
            tail_block(which, lambda i: i),
        ],
        out_specs=whole(frames, PIX, CH),
        out_shape=jax.ShapeDtypeStruct((frames, PIX, CH), F32),
        scratch_shapes=[pltpu.VMEM((frames, PIX + 2 * SIDE, 3 * CH), BF16)],
        compiler_params=params(20),
        cost_estimate=cost(11 * frames, 12),
        name="conv_second",
    )(activated, second)
    return pl.pallas_call(
        last_kernel,
        grid=(1,),
        in_specs=[
            whole(frames, PIX, CH),
            whole(frames, PIX, CH),
            whole(PIX, CH),
            whole(PIX, CH),
            tail_block(which, lambda i: 3),
        ],
        out_specs=whole(frames, PIX, CH),
        out_shape=jax.ShapeDtypeStruct((frames, PIX, CH), BF16),
        compiler_params=params(20),
        cost_estimate=cost(2, 3),
        name="halo_and_residual",
    )(acc, e, left, right, second)


def joined(h, skip):
    return ((h.astype(F32) + skip.astype(F32)) * skip_scale).astype(BF16)


def spread_clips(noisy):
    zlo, core, x = lax.axis_index("zlo"), lax.axis_index("core"), lax.axis_index("x")
    clips = noisy.reshape(4, PIX, CH)
    got = []
    for r in range(2):
        clip = lax.dynamic_index_in_dim(clips, 2 * zlo + (r ^ core), 0, keepdims=False)

        def route(sx, sy, sz, sc, r=r):
            hi, lo = sz // 2, sz % 2
            return (2 * lo + (r ^ sc), sy, 2 * sx + hi // 2, hi % 2)

        got.append(sent(clip, route))
    even = x % 2 == 0
    return jnp.stack([jnp.where(even, got[0], got[1]), jnp.where(even, got[1], got[0])])


def deliver(h):
    y, zlo, core, x = (lax.axis_index(n) for n in ("y", "zlo", "core", "x"))
    rows = h.reshape(2, NY, 2, 2, SIDE, CH)
    mine = rows[:, NY - 1]
    for target in range(NY - 1):
        got = sent(rows[:, target], plane_to_plane(NY - 1, target))
        mine = jnp.where(y == target, got, mine)
    messages = mine.reshape(4, 2, SIDE, CH)
    slots = []
    for r in range(4):
        message = lax.dynamic_index_in_dim(messages, x ^ r, 0, keepdims=False)

        def route(sx, sy, sz, sc, r=r):
            k, lo = (sx ^ r) // 2, (sx ^ r) % 2
            return (sz // 2, sy, 2 * (2 * (sz % 2) + sc) + lo, k)

        slots.append(sent(message, route))
    slots = jnp.stack(slots)
    here = core * 2 + zlo
    out = [lax.dynamic_index_in_dim(slots, here ^ c, 0, keepdims=False) for c in range(4)]
    return jnp.stack(out)[:, None]


def put(buffer, piece, *start):
    return lax.dynamic_update_slice(buffer, piece, start)


def gathered(conv_first, conv_second, temporal):
    x, zhi, zlo, core = (lax.axis_index(n).astype(jnp.uint32) for n in ("x", "zhi", "zlo", "core"))
    z = 2 * zhi + zlo
    zero = jnp.uint32(0)

    tail = jnp.concatenate([conv_second, temporal], axis=0)
    taps = tail.shape[0]
    by_z = [(tail, 0)]
    right = left = tail
    for d in range(1, 5):
        right = sent(right, along(0, 1))
        by_z.append((right, -d))
        if d < 4:
            left = sent(left, along(0, -1))
            by_z.append((left, d))
    tails = jnp.zeros((taps, 2, NZ // 2, 16, CH), BF16)
    for piece, offset in by_z:
        source = (z + np.uint32(offset % NZ)) & np.uint32(NZ - 1)
        tails = put(tails, piece.reshape(taps, 1, 1, 16, CH), zero, source & 1, source >> 1, zero, zero)
    second = lax.all_gather(tails, ("x", "core"), axis=0, tiled=False)
    second = second.reshape(NX, 2, taps, 2, NZ // 2, 16, CH)

    right = sent(conv_first, along(1, 0))
    left = sent(conv_first, along(-1, 0))
    far = sent(right, along(1, 0))
    row = jnp.zeros((9, NX, 16, CH), BF16)
    for piece, offset in ((conv_first, 0), (right, -1), (left, 1), (far, 2)):
        row = put(row, piece.reshape(9, 1, 16, CH), zero, (x + np.uint32(offset % NX)) & np.uint32(NX - 1), zero, zero)

    pieces = [(row, 0, 0)]
    right = left = row
    for d in range(1, 4):
        right, left = sent(right, along(0, 1)), sent(left, along(0, -1))
        pieces += [(right, -d, 0), (left, d, 0)]
    half = NX // 2
    pieces.append((sent(right[:, :half], along(0, 1)), 4, 0))
    pieces.append((sent(left[:, half:], along(0, -1)), 4, half))
    first = jnp.zeros((9, 2, NX, NZ // 2, 2, 16, CH), BF16)
    for piece, offset, start in pieces:
        source = (z + np.uint32(offset % NZ)) & np.uint32(NZ - 1)
        for block, owner in ((piece, core), (sent(piece, other_core), core ^ 1)):
            block = block.reshape(9, 1, -1, 1, 1, 16, CH)
            at = (zero, source & 1, jnp.uint32(start), source >> 1, owner, zero, zero)
            first = put(first, block, *at)
    return first.reshape(9, 2 * CH, CH), second


def on_device(noisy, conv_first, conv_second, temporal):
    first, second = gathered(conv_first[0], conv_second[0], temporal[0])
    e0 = spread_clips(noisy)
    e1 = section(e0, first, second, 0)
    skip6 = sent(e1, plane_to_plane(0, 3))
    h = section(e1, first, second, 1)
    e2 = sent(h, plane_to_plane(0, 1))
    skip5 = sent(e2, plane_to_plane(1, 2))
    e3 = section(e2, first, second, 0)
    h = section(e3, first, second, 1)
    e4 = sent(joined(h, e3), plane_to_plane(1, 2))
    h = section(e4, first, second, 0)
    h = section(joined(h, skip5), first, second, 1)
    h = sent(h, plane_to_plane(2, 3))
    h = section(joined(h, skip6), first, second, 0)
    h = section(joined(h, e0), first, second, 1)
    return deliver(h)


def solution(mesh):
    fine = Mesh(mesh.devices.reshape(NY, 2, NX, NZ // 2, 2), AXES)
    weight_spec = P(SEGMENT, None, FRAME, None)
    return jax.shard_map(
        on_device,
        mesh=fine,
        in_specs=(P(None, FRAME), weight_spec, weight_spec, weight_spec),
        out_specs=P(None, FRAME, SEGMENT),
        check_vma=False,
    )
```

```python
import functools
import itertools

import jax
import jax.numpy as jnp
import numpy as np
from jax import lax
from jax.experimental import pallas as pl
from jax.experimental.pallas import tpu as pltpu
from jax.sharding import Mesh
from jax.sharding import PartitionSpec as P

skip_scale = 0.7071067811865476
AXES = ("y", "zlo", "x", "zhi", "core")
SEGMENT = ("y", "zlo")
FRAME = ("x", "zhi", "core")
PLANE = ("zlo", "x", "zhi", "core")
NY, NX, NZ = 4, 4, 8
SIDE = 16
CH = 512
PIX = SIDE * SIDE
F32 = jnp.float32
BF16 = jnp.bfloat16


def flat(x, y, z, core):
    return (((y * 2 + z % 2) * 4 + x) * 4 + z // 2) * 2 + core


def sent(value, route):
    pairs = []
    for x, y, z, core in itertools.product(range(NX), range(NY), range(NZ), range(2)):
        target = route(x, y, z, core)
        if target is not None:
            pairs.append((flat(x, y, z, core), flat(*target)))
    return lax.ppermute(value, AXES, pairs)


def outward(x, y, z, core):
    partner = z + 2 * core - 1
    return (x, y, partner, 1 - core) if 0 <= partner < NZ else None


def along(dx, dz):
    return lambda x, y, z, core: ((x + dx) % NX, y, (z + dz) % NZ, core)


def other_core(x, y, z, core):
    return (x, y, z, 1 - core)


def plane_to_plane(source, target):
    return lambda x, y, z, core: (x, target, z, core) if y == source else None


def silu(u):
    return u / (1.0 + jnp.exp(-u))


def widen(frame, wide_ref, index):
    full = frame.astype(F32)
    column = lax.broadcasted_iota(jnp.int32, (PIX, CH), 0) % SIDE
    before = jnp.where(column == 0, 0.0, pltpu.roll(full, 1, 0)).astype(BF16)
    after = jnp.where(column == SIDE - 1, 0.0, pltpu.roll(full, PIX - 1, 0)).astype(BF16)
    edge = jnp.zeros((SIDE, 3 * CH), BF16)
    wide_ref[index, 0:SIDE, :] = edge
    wide_ref[index, SIDE + PIX : 2 * SIDE + PIX, :] = edge
    wide_ref[index, SIDE : SIDE + PIX, 0:CH] = before
    wide_ref[index, SIDE : SIDE + PIX, CH : 2 * CH] = frame
    wide_ref[index, SIDE : SIDE + PIX, 2 * CH : 3 * CH] = after


def conv(wide_ref, index, weights_of):
    total = None
    for dy in range(3):
        rows = wide_ref[index, dy * SIDE : dy * SIDE + PIX, :]
        part = jnp.dot(rows, weights_of(dy), preferred_element_type=F32)
        total = part if total is None else total + part
    return total


def stacked_taps(w_ref, which, taps):
    order = itertools.product(taps, range(NX), range(NZ // 2), range(2))
    return jnp.concatenate([w_ref[x, core, t, which, hi] for t, x, hi, core in order], axis=0)


def first_kernel(which, outer_ref, inner_ref, w_ref, outer_out, inner_out, wide_ref):
    widen(outer_ref[...], wide_ref, 0)
    widen(inner_ref[...], wide_ref, 1)

    def weights_of(dy):
        return w_ref[3 * dy : 3 * dy + 3, which * CH : (which + 1) * CH, :].reshape(3 * CH, CH)

    @pl.loop(0, 2)
    def _(i):
        out = silu(conv(wide_ref, i, weights_of)).astype(BF16)

        @pl.when(i == 0)
        def _():
            outer_out[...] = out

        @pl.when(i == 1)
        def _():
            inner_out[...] = out


def second_kernel(which, core_ref, outer_ref, inner_ref, w_ref, acc_ref, wide_ref):
    widen(outer_ref[...], wide_ref, 0)
    widen(inner_ref[...], wide_ref, 1)
    core = core_ref[0]

    @pl.loop(0, 2)
    def _(i):
        total = conv(wide_ref, i, lambda dy: stacked_taps(w_ref, which, range(3 * dy, 3 * dy + 3)))
        own = wide_ref[i, SIDE : SIDE + PIX, CH : 2 * CH]
        total += jnp.dot(own, stacked_taps(w_ref, which, [10]), preferred_element_type=F32)
        other = wide_ref[1 - i, SIDE : SIDE + PIX, CH : 2 * CH]
        tap = 11 - 2 * (core ^ i)
        total += jnp.dot(other, stacked_taps(w_ref, which, [tap]), preferred_element_type=F32)
        acc_ref[i] = total


def last_kernel(which, core_ref, acc_ref, outer_ref, inner_ref, cross_ref, near_ref, w_ref, outer_out, inner_out):
    core = core_ref[0]
    sides = ((outer_ref, cross_ref, outer_out), (inner_ref, near_ref, inner_out))
    for i, (e_ref, beyond_ref, out_ref) in enumerate(sides):
        weights = stacked_taps(w_ref, which, [9 + 2 * (core ^ i)])
        total = acc_ref[i] + jnp.dot(beyond_ref[...], weights, preferred_element_type=F32)
        out_ref[...] = (e_ref[...].astype(F32) + silu(total)).astype(BF16)


VM = pl.BlockSpec(memory_space=pltpu.VMEM)
SM = pl.BlockSpec(memory_space=pltpu.SMEM)
FRAME_OUT = jax.ShapeDtypeStruct((PIX, CH), BF16)
WIDE = pltpu.VMEM((2, PIX + 2 * SIDE, 3 * CH), BF16)


def call(kernel, which, in_specs, out_shape, scratch, taps, name):
    return pl.pallas_call(
        functools.partial(kernel, which),
        in_specs=in_specs,
        out_specs=jax.tree.map(lambda _: VM, out_shape),
        out_shape=out_shape,
        scratch_shapes=scratch,
        compiler_params=pltpu.CompilerParams(vmem_limit_bytes=16 << 20),
        cost_estimate=pl.CostEstimate(
            flops=2 * taps * PIX * CH * CH, bytes_accessed=8 * PIX * CH, transcendentals=2 * PIX * CH
        ),
        name=name,
    )


def section(e, first, second, core, which):
    a = call(first_kernel, which, [VM] * 3, (FRAME_OUT,) * 2, [WIDE], 18, "conv_first")(*e, first)
    cross, near = sent(a[0], outward), sent(a[1], other_core)
    acc_shape = jax.ShapeDtypeStruct((2, PIX, CH), F32)
    acc = call(second_kernel, which, [SM] + [VM] * 3, acc_shape, [WIDE], 22, "conv_second")(core, *a, second)
    last = call(last_kernel, which, [SM] + [VM] * 6, (FRAME_OUT,) * 2, [], 2, "halo_and_residual")
    return last(core, acc, *e, cross, near, second)


def joined(h, skip):
    return tuple(((a.astype(F32) + b.astype(F32)) * skip_scale).astype(BF16) for a, b in zip(h, skip))


def hop(frames, source, target):
    return tuple(sent(f, plane_to_plane(source, target)) for f in frames)


def spread_clips(noisy):
    y, zlo, core, x = (lax.axis_index(n) for n in ("y", "zlo", "core", "x"))
    clips = noisy.reshape(4, PIX, CH)
    got = []
    for r in range(2):
        clip = lax.dynamic_index_in_dim(clips, 2 * zlo + (r ^ core), 0, keepdims=False)

        def route(sx, sy, sz, sc, r=r):
            hi, lo = sz // 2, sz % 2
            return (2 * lo + (r ^ sc), sy, 2 * sx + hi // 2, hi % 2) if sy % 2 else None

        got.append(sent(clip, route))
    even = (x ^ core) % 2 == 0
    frames = jnp.where(even, got[0], got[1]), jnp.where(even, got[1], got[0])
    return tuple(jnp.where(y == 0, g, f) for g, f in zip(hop(frames, 1, 0), frames))


def deliver(h):
    y, zlo, core, x = (lax.axis_index(n) for n in ("y", "zlo", "core", "x"))
    rows = jnp.stack(h).reshape(2, NY, 2, 2, SIDE, CH)
    mine = rows[:, NY - 1]
    for target in range(NY - 1):
        got = sent(rows[:, target], plane_to_plane(NY - 1, target))
        mine = jnp.where(y == target, got, mine)
    messages = mine.reshape(4, 2, SIDE, CH)
    slots = []
    for r in range(4):
        message = lax.dynamic_index_in_dim(messages, x ^ r ^ (2 * core), 0, keepdims=False)

        def route(sx, sy, sz, sc, r=r):
            k, lo = (sx ^ r) // 2, (sx ^ r) % 2
            return (sz // 2, sy, 2 * (2 * (sz % 2) + sc) + lo, k)

        slots.append(sent(message, route))
    slots = jnp.stack(slots)
    here = core * 2 + zlo
    out = [lax.dynamic_index_in_dim(slots, here ^ c, 0, keepdims=False) for c in range(4)]
    return jnp.stack(out)[:, None]


def put(buffer, piece, *start):
    return lax.dynamic_update_slice(buffer, piece, start)


def gathered(conv_first, conv_second, temporal):
    x, zhi, zlo, core = (lax.axis_index(n).astype(jnp.uint32) for n in ("x", "zhi", "zlo", "core"))
    z = 2 * zhi + zlo
    zero = jnp.uint32(0)

    right = sent(conv_first, along(1, 0))
    left = sent(conv_first, along(-1, 0))
    far = sent(right, along(1, 0))
    row = jnp.zeros((9, NX, 16, CH), BF16)
    for piece, offset in ((conv_first, 0), (right, -1), (left, 1), (far, 2)):
        row = put(row, piece.reshape(9, 1, 16, CH), zero, (x + np.uint32(offset % NX)) & np.uint32(NX - 1), zero, zero)

    tail = jnp.concatenate([conv_second, temporal], axis=0)
    taps = tail.shape[0]
    by_z = [(tail, 0)]
    right = left = tail
    for d in range(1, 5):
        right = sent(right, along(0, 1))
        by_z.append((right, -d))
        if d < 4:
            left = sent(left, along(0, -1))
            by_z.append((left, d))
    tails = jnp.zeros((taps, 2, NZ // 2, 16, CH), BF16)
    for piece, offset in by_z:
        source = (z + np.uint32(offset % NZ)) & np.uint32(NZ - 1)
        tails = put(tails, piece.reshape(taps, 1, 1, 16, CH), zero, source & 1, source >> 1, zero, zero)
    tails, row = lax.optimization_barrier((tails, row))
    second = lax.all_gather(tails, ("x", "core"), axis=0, tiled=False)
    second = second.reshape(NX, 2, taps, 2, NZ // 2, 16, CH)

    pieces = [(row, 0, 0)]
    right = left = row
    for d in range(1, 4):
        right, left = sent(right, along(0, 1)), sent(left, along(0, -1))
        pieces += [(right, -d, 0), (left, d, 0)]
    half = NX // 2
    pieces.append((sent(right[:, :half], along(0, 1)), 4, 0))
    pieces.append((sent(left[:, half:], along(0, -1)), 4, half))
    first = jnp.zeros((9, 2, NX, NZ // 2, 2, 16, CH), BF16)
    for piece, offset, start in pieces:
        source = (z + np.uint32(offset % NZ)) & np.uint32(NZ - 1)
        for block, owner in ((piece, core), (sent(piece, other_core), core ^ 1)):
            block = block.reshape(9, 1, -1, 1, 1, 16, CH)
            at = (zero, source & 1, jnp.uint32(start), source >> 1, owner, zero, zero)
            first = put(first, block, *at)
    return first.reshape(9, 2 * CH, CH), second


def on_device(noisy, conv_first, conv_second, temporal):
    first, second = gathered(conv_first[0], conv_second[0], temporal[0])
    core = lax.axis_index("core").astype(jnp.int32).reshape(1)

    def run(e, which):
        return section(e, first, second, core, which)

    e0 = spread_clips(noisy)
    e1 = run(e0, 0)
    skip6 = hop(e1, 0, 3)
    e2 = hop(run(e1, 1), 0, 1)
    skip5 = hop(e2, 1, 2)
    e3 = run(e2, 0)
    e4 = hop(joined(run(e3, 1), e3), 1, 2)
    h = run(e4, 0)
    h = hop(run(joined(h, skip5), 1), 2, 3)
    h = run(joined(h, skip6), 0)
    h = run(joined(h, e0), 1)
    return deliver(h)


def solution(mesh):
    fine = Mesh(mesh.devices.reshape(NY, 2, NX, NZ // 2, 2), AXES)
    weight_spec = P(SEGMENT, None, FRAME, None)
    return jax.shard_map(
        on_device,
        mesh=fine,
        in_specs=(P(None, FRAME), weight_spec, weight_spec, weight_spec),
        out_specs=P(None, FRAME, SEGMENT),
        check_vma=False,
    )
```

```python
import functools
import itertools

import jax
import jax.numpy as jnp
import numpy as np
from jax import lax
from jax.experimental import pallas as pl
from jax.experimental.pallas import tpu as pltpu
from jax.sharding import Mesh
from jax.sharding import PartitionSpec as P

skip_scale = 0.7071067811865476
AXES = ("y", "zlo", "x", "zhi", "core")
SEGMENT = ("y", "zlo")
FRAME = ("x", "zhi", "core")
PLANE = ("zlo", "x", "zhi", "core")
NY, NX, NZ = 4, 4, 8
SIDE = 16
CH = 512
PIX = SIDE * SIDE
F32 = jnp.float32
BF16 = jnp.bfloat16


def flat(x, y, z, core):
    return (((y * 2 + z % 2) * 4 + x) * 4 + z // 2) * 2 + core


def sent(value, route):
    pairs = []
    for x, y, z, core in itertools.product(range(NX), range(NY), range(NZ), range(2)):
        target = route(x, y, z, core)
        if target is not None:
            pairs.append((flat(x, y, z, core), flat(*target)))
    return lax.ppermute(value, AXES, pairs)


def outward(x, y, z, core):
    partner = z + 2 * core - 1
    return (x, y, partner, 1 - core) if 0 <= partner < NZ else None


def along(dx, dz):
    return lambda x, y, z, core: ((x + dx) % NX, y, (z + dz) % NZ, core)


def other_core(x, y, z, core):
    return (x, y, z, 1 - core)


def plane_to_plane(source, target):
    return lambda x, y, z, core: (x, target, z, core) if y == source else None


def silu(u):
    return u / (1.0 + jnp.exp(-u))


def widen(frame, wide_ref, index):
    full = frame.astype(F32)
    column = lax.broadcasted_iota(jnp.int32, (PIX, CH), 0) % SIDE
    before = jnp.where(column == 0, 0.0, pltpu.roll(full, 1, 0)).astype(BF16)
    after = jnp.where(column == SIDE - 1, 0.0, pltpu.roll(full, PIX - 1, 0)).astype(BF16)
    edge = jnp.zeros((SIDE, 3 * CH), BF16)
    wide_ref[index, 0:SIDE, :] = edge
    wide_ref[index, SIDE + PIX : 2 * SIDE + PIX, :] = edge
    wide_ref[index, SIDE : SIDE + PIX, 0:CH] = before
    wide_ref[index, SIDE : SIDE + PIX, CH : 2 * CH] = frame
    wide_ref[index, SIDE : SIDE + PIX, 2 * CH : 3 * CH] = after


def conv(wide_ref, index, weights_of):
    total = None
    for dy in range(3):
        rows = wide_ref[index, dy * SIDE : dy * SIDE + PIX, :]
        part = jnp.dot(rows, weights_of(dy), preferred_element_type=F32)
        total = part if total is None else total + part
    return total


def stacked_taps(w_ref, which, taps):
    order = itertools.product(taps, range(NX), range(NZ // 2), range(2))
    return jnp.concatenate([w_ref[x, core, t, which, hi] for t, x, hi, core in order], axis=0)


def first_kernel(which, outer_ref, inner_ref, w_ref, outer_out, inner_out, wide_ref):
    widen(outer_ref[...], wide_ref, 0)
    widen(inner_ref[...], wide_ref, 1)

    def weights_of(dy):
        return w_ref[3 * dy : 3 * dy + 3, which * CH : (which + 1) * CH, :].reshape(3 * CH, CH)

    @pl.loop(0, 2)
    def _(i):
        out = silu(conv(wide_ref, i, weights_of)).astype(BF16)

        @pl.when(i == 0)
        def _():
            outer_out[...] = out

        @pl.when(i == 1)
        def _():
            inner_out[...] = out


def second_kernel(which, core_ref, outer_ref, inner_ref, w_ref, acc_ref, wide_ref):
    widen(outer_ref[...], wide_ref, 0)
    widen(inner_ref[...], wide_ref, 1)
    core = core_ref[0]

    @pl.loop(0, 2)
    def _(i):
        total = conv(wide_ref, i, lambda dy: stacked_taps(w_ref, which, range(3 * dy, 3 * dy + 3)))
        own = wide_ref[i, SIDE : SIDE + PIX, CH : 2 * CH]
        total += jnp.dot(own, stacked_taps(w_ref, which, [10]), preferred_element_type=F32)
        other = wide_ref[1 - i, SIDE : SIDE + PIX, CH : 2 * CH]
        tap = 11 - 2 * (core ^ i)
        total += jnp.dot(other, stacked_taps(w_ref, which, [tap]), preferred_element_type=F32)
        acc_ref[i] = total


def last_kernel(which, core_ref, acc_ref, outer_ref, inner_ref, cross_ref, near_ref, w_ref, outer_out, inner_out):
    core = core_ref[0]
    sides = ((outer_ref, cross_ref, outer_out), (inner_ref, near_ref, inner_out))
    for i, (e_ref, beyond_ref, out_ref) in enumerate(sides):
        weights = stacked_taps(w_ref, which, [9 + 2 * (core ^ i)])
        total = acc_ref[i] + jnp.dot(beyond_ref[...], weights, preferred_element_type=F32)
        out_ref[...] = (e_ref[...].astype(F32) + silu(total)).astype(BF16)


VM = pl.BlockSpec(memory_space=pltpu.VMEM)
SM = pl.BlockSpec(memory_space=pltpu.SMEM)
FRAME_OUT = jax.ShapeDtypeStruct((PIX, CH), BF16)
WIDE = pltpu.VMEM((2, PIX + 2 * SIDE, 3 * CH), BF16)


def call(kernel, which, in_specs, out_shape, scratch, taps, name):
    return pl.pallas_call(
        functools.partial(kernel, which),
        in_specs=in_specs,
        out_specs=jax.tree.map(lambda _: VM, out_shape),
        out_shape=out_shape,
        scratch_shapes=scratch,
        compiler_params=pltpu.CompilerParams(vmem_limit_bytes=8 << 20),
        cost_estimate=pl.CostEstimate(
            flops=2 * taps * PIX * CH * CH, bytes_accessed=8 * PIX * CH, transcendentals=2 * PIX * CH
        ),
        name=name,
    )


def section(e, first, second, core, which):
    a = call(first_kernel, which, [VM] * 3, (FRAME_OUT,) * 2, [WIDE], 18, "conv_first")(*e, first)
    near, outer = lax.optimization_barrier((sent(a[1], other_core), a[0]))
    cross = sent(outer, outward)
    acc_shape = jax.ShapeDtypeStruct((2, PIX, CH), F32)
    acc = call(second_kernel, which, [SM] + [VM] * 3, acc_shape, [WIDE], 22, "conv_second")(core, *a, second)
    last = call(last_kernel, which, [SM] + [VM] * 6, (FRAME_OUT,) * 2, [], 2, "halo_and_residual")
    return last(core, acc, *e, cross, near, second)


def joined(h, skip):
    return tuple(((a.astype(F32) + b.astype(F32)) * skip_scale).astype(BF16) for a, b in zip(h, skip))


def hop(frames, source, target):
    return tuple(sent(f, plane_to_plane(source, target)) for f in frames)


def spread_clips(noisy):
    zlo, core, x = (lax.axis_index(n) for n in ("zlo", "core", "x"))
    clips = noisy.reshape(4, PIX, CH)
    got = []
    for r in range(2):
        clip = lax.dynamic_index_in_dim(clips, 2 * zlo + (r ^ core), 0, keepdims=False)

        def route(sx, sy, sz, sc, r=r):
            hi, lo = sz // 2, sz % 2
            return (2 * lo + (r ^ sc), sy, 2 * sx + hi // 2, hi % 2) if sy % 2 else None

        got.append(sent(clip, route))
    even = (x ^ core) % 2 == 0
    frames = jnp.where(even, got[0], got[1]), jnp.where(even, got[1], got[0])
    return frames, hop(frames, 1, 0)


def deliver(h):
    y, zlo, core, x = (lax.axis_index(n) for n in ("y", "zlo", "core", "x"))
    rows = jnp.stack(h).reshape(2, NY, 2, 2, SIDE, CH)
    mine = rows[:, NY - 1]
    for target in range(NY - 1):
        got = sent(rows[:, target], plane_to_plane(NY - 1, target))
        mine = jnp.where(y == target, got, mine)
    def to_owner(sx, sy, sz, sc):
        return (sz // 2, sy, 2 * (2 * (sz % 2) + sc) + sx % 2, sx // 2)

    def other_chip(sx, sy, sz, sc):
        return (sx, sy, sz ^ 1, sc)

    natural = jnp.where(core == 0, mine, mine[::-1])
    held = sent(natural, to_owner)
    got = sent(lax.dynamic_index_in_dim(held, 1 - core, 0, keepdims=False), other_core)
    kept = lax.dynamic_index_in_dim(held, core, 0, keepdims=False)
    by_core = jnp.stack([jnp.where(core == 0, kept, got), jnp.where(core == 0, got, kept)])
    got = sent(lax.dynamic_index_in_dim(by_core, 1 - zlo, 1, keepdims=False), other_chip)
    kept = lax.dynamic_index_in_dim(by_core, zlo, 1, keepdims=False)
    even, odd = jnp.where(zlo == 0, kept, got), jnp.where(zlo == 0, got, kept)
    return jnp.stack([even, odd], axis=1).reshape(4, 1, 2, SIDE, CH)


def put(buffer, piece, *start):
    return lax.dynamic_update_slice(buffer, piece, start)


def gathered(conv_first, conv_second, temporal):
    x, zhi, zlo, core = (lax.axis_index(n).astype(jnp.uint32) for n in ("x", "zhi", "zlo", "core"))
    z = 2 * zhi + zlo
    zero = jnp.uint32(0)

    right = sent(conv_first, along(1, 0))
    left = sent(conv_first, along(-1, 0))
    far = sent(right, along(1, 0))
    row = jnp.zeros((9, NX, 16, CH), BF16)
    for piece, offset in ((conv_first, 0), (right, -1), (left, 1), (far, 2)):
        row = put(row, piece.reshape(9, 1, 16, CH), zero, (x + np.uint32(offset % NX)) & np.uint32(NX - 1), zero, zero)

    tail = jnp.concatenate([conv_second, temporal], axis=0)
    taps = tail.shape[0]
    by_z = [(tail, 0)]
    right = left = tail
    for d in range(1, 5):
        right = sent(right, along(0, 1))
        by_z.append((right, -d))
        if d < 4:
            left = sent(left, along(0, -1))
            by_z.append((left, d))
    tails = jnp.zeros((taps, 2, NZ // 2, 16, CH), BF16)
    for piece, offset in by_z:
        source = (z + np.uint32(offset % NZ)) & np.uint32(NZ - 1)
        tails = put(tails, piece.reshape(taps, 1, 1, 16, CH), zero, source & 1, source >> 1, zero, zero)
    tails, row = lax.optimization_barrier((tails, row))
    second = lax.all_gather(tails, ("x", "core"), axis=0, tiled=False)
    second = second.reshape(NX, 2, taps, 2, NZ // 2, 16, CH)

    pieces = [(row, 0, 0)]
    right = left = row
    for d in range(1, 4):
        right, left = sent(right, along(0, 1)), sent(left, along(0, -1))
        pieces += [(right, -d, 0), (left, d, 0)]
    half = NX // 2
    pieces.append((sent(right[:, :half], along(0, 1)), 4, 0))
    pieces.append((sent(left[:, half:], along(0, -1)), 4, half))
    first = jnp.zeros((9, 2, NX, NZ // 2, 2, 16, CH), BF16)
    for piece, offset, start in pieces:
        source = (z + np.uint32(offset % NZ)) & np.uint32(NZ - 1)
        for block, owner in ((piece, core), (sent(piece, other_core), core ^ 1)):
            block = block.reshape(9, 1, -1, 1, 1, 16, CH)
            at = (zero, source & 1, jnp.uint32(start), source >> 1, owner, zero, zero)
            first = put(first, block, *at)
    return first.reshape(9, 2 * CH, CH), second


def on_device(noisy, conv_first, conv_second, temporal):
    frames, passed = spread_clips(noisy)
    first, second = gathered(conv_first[0], conv_second[0], temporal[0])
    first, frames, passed = lax.optimization_barrier((first, frames, passed))
    e0 = tuple(jnp.where(lax.axis_index("y") == 0, p, f) for p, f in zip(passed, frames))
    core = lax.axis_index("core").astype(jnp.int32).reshape(1)

    def run(e, which):
        return section(e, first, second, core, which)

    e1 = run(e0, 0)
    skip6 = hop(e1, 0, 3)
    e2 = hop(run(e1, 1), 0, 1)
    skip5 = hop(e2, 1, 2)
    e3 = run(e2, 0)
    e4 = hop(joined(run(e3, 1), e3), 1, 2)
    h = run(e4, 0)
    h = hop(run(joined(h, skip5), 1), 2, 3)
    h = run(joined(h, skip6), 0)
    h = run(joined(h, e0), 1)
    return deliver(h)


def solution(mesh):
    fine = Mesh(mesh.devices.reshape(NY, 2, NX, NZ // 2, 2), AXES)
    weight_spec = P(SEGMENT, None, FRAME, None)
    return jax.shard_map(
        on_device,
        mesh=fine,
        in_specs=(P(None, FRAME), weight_spec, weight_spec, weight_spec),
        out_specs=P(None, FRAME, SEGMENT),
        check_vma=False,
    )
```

```python
import functools
import itertools

import jax
import jax.numpy as jnp
import numpy as np
from jax import lax
from jax.experimental import pallas as pl
from jax.experimental.pallas import tpu as pltpu
from jax.sharding import Mesh
from jax.sharding import PartitionSpec as P

skip_scale = 0.7071067811865476
AXES = ("y", "zlo", "x", "zhi", "core")
SEGMENT = ("y", "zlo")
FRAME = ("x", "zhi", "core")
PLANE = ("zlo", "x", "zhi", "core")
NY, NX, NZ = 4, 4, 8
SIDE = 16
CH = 512
PIX = SIDE * SIDE
F32 = jnp.float32
BF16 = jnp.bfloat16


def flat(x, y, z, core):
    return (((y * 2 + z % 2) * 4 + x) * 4 + z // 2) * 2 + core


def sent(value, route):
    pairs = []
    for x, y, z, core in itertools.product(range(NX), range(NY), range(NZ), range(2)):
        target = route(x, y, z, core)
        if target is not None:
            pairs.append((flat(x, y, z, core), flat(*target)))
    return lax.ppermute(value, AXES, pairs)


def block_of(x, z):
    return (z + 2 * x) % NZ


def outward(x, y, z, core):
    step = 2 * core - 1
    return (x, y, (z + step) % NZ, 1 - core) if 0 <= block_of(x, z) + step < NZ else None


def along(dx, dz):
    return lambda x, y, z, core: ((x + dx) % NX, y, (z + dz) % NZ, core)


def other_core(x, y, z, core):
    return (x, y, z, 1 - core)


def plane_to_plane(source, target):
    return lambda x, y, z, core: (x, target, z, core) if y == source else None


def silu(u):
    return u / (1.0 + jnp.exp(-u))


def widen(frame, wide_ref, index):
    full = frame.astype(F32)
    column = lax.broadcasted_iota(jnp.int32, (PIX, CH), 0) % SIDE
    before = jnp.where(column == 0, 0.0, pltpu.roll(full, 1, 0)).astype(BF16)
    after = jnp.where(column == SIDE - 1, 0.0, pltpu.roll(full, PIX - 1, 0)).astype(BF16)
    edge = jnp.zeros((SIDE, 3 * CH), BF16)
    wide_ref[index, 0:SIDE, :] = edge
    wide_ref[index, SIDE + PIX : 2 * SIDE + PIX, :] = edge
    wide_ref[index, SIDE : SIDE + PIX, 0:CH] = before
    wide_ref[index, SIDE : SIDE + PIX, CH : 2 * CH] = frame
    wide_ref[index, SIDE : SIDE + PIX, 2 * CH : 3 * CH] = after


def conv(wide_ref, index, weights_of):
    total = None
    for dy in range(3):
        rows = wide_ref[index, dy * SIDE : dy * SIDE + PIX, :]
        part = jnp.dot(rows, weights_of(dy), preferred_element_type=F32)
        total = part if total is None else total + part
    return total


def stacked_taps(w_ref, which, taps):
    order = itertools.product(taps, range(NX), range(NZ // 2), range(2))
    return jnp.concatenate([w_ref[x, core, t, which, hi] for t, x, hi, core in order], axis=0)


def first_kernel(which, outer_ref, inner_ref, w_ref, outer_out, inner_out, wide_ref):
    widen(outer_ref[...], wide_ref, 0)
    widen(inner_ref[...], wide_ref, 1)

    def weights_of(dy):
        return w_ref[3 * dy : 3 * dy + 3, which * CH : (which + 1) * CH, :].reshape(3 * CH, CH)

    @pl.loop(0, 2)
    def _(i):
        out = silu(conv(wide_ref, i, weights_of)).astype(BF16)

        @pl.when(i == 0)
        def _():
            outer_out[...] = out

        @pl.when(i == 1)
        def _():
            inner_out[...] = out


def second_kernel(which, core_ref, outer_ref, inner_ref, middle_ref, w_ref, acc_ref, wide_ref):
    widen(outer_ref[...], wide_ref, 0)
    widen(inner_ref[...], wide_ref, 1)
    core = core_ref[0]

    @pl.loop(0, 2)
    def _(i):
        total = conv(wide_ref, i, lambda dy: stacked_taps(w_ref, which, range(3 * dy, 3 * dy + 3)))
        own = wide_ref[i, SIDE : SIDE + PIX, CH : 2 * CH]
        middle = middle_ref[which * CH : (which + 1) * CH, :]
        total += jnp.dot(own, middle, preferred_element_type=F32)
        other = wide_ref[1 - i, SIDE : SIDE + PIX, CH : 2 * CH]
        tap = 10 - (core ^ i)
        total += jnp.dot(other, stacked_taps(w_ref, which, [tap]), preferred_element_type=F32)
        acc_ref[i] = total


def last_kernel(which, core_ref, acc_ref, outer_ref, inner_ref, cross_ref, near_ref, w_ref, outer_out, inner_out):
    core = core_ref[0]
    sides = ((outer_ref, cross_ref, outer_out), (inner_ref, near_ref, inner_out))
    for i, (e_ref, beyond_ref, out_ref) in enumerate(sides):
        weights = stacked_taps(w_ref, which, [9 + (core ^ i)])
        total = acc_ref[i] + jnp.dot(beyond_ref[...], weights, preferred_element_type=F32)
        out_ref[...] = (e_ref[...].astype(F32) + silu(total)).astype(BF16)


VM = pl.BlockSpec(memory_space=pltpu.VMEM)
SM = pl.BlockSpec(memory_space=pltpu.SMEM)
FRAME_OUT = jax.ShapeDtypeStruct((PIX, CH), BF16)
WIDE = pltpu.VMEM((2, PIX + 2 * SIDE, 3 * CH), BF16)


def call(kernel, which, in_specs, out_shape, scratch, taps, name):
    return pl.pallas_call(
        functools.partial(kernel, which),
        in_specs=in_specs,
        out_specs=jax.tree.map(lambda _: VM, out_shape),
        out_shape=out_shape,
        scratch_shapes=scratch,
        compiler_params=pltpu.CompilerParams(vmem_limit_bytes=8 << 20),
        cost_estimate=pl.CostEstimate(
            flops=2 * taps * PIX * CH * CH, bytes_accessed=8 * PIX * CH, transcendentals=2 * PIX * CH
        ),
        name=name,
    )


def section(e, first, middle, second, core, which):
    a = call(first_kernel, which, [VM] * 3, (FRAME_OUT,) * 2, [WIDE], 18, "conv_first")(*e, first)
    cross, near = sent(a[0], outward), sent(a[1], other_core)
    acc_shape = jax.ShapeDtypeStruct((2, PIX, CH), F32)
    acc = call(second_kernel, which, [SM] + [VM] * 4, acc_shape, [WIDE], 22, "conv_second")(core, *a, middle, second)
    last = call(last_kernel, which, [SM] + [VM] * 6, (FRAME_OUT,) * 2, [], 2, "halo_and_residual")
    return last(core, acc, *e, cross, near, second)


def joined(h, skip):
    return tuple(((a.astype(F32) + b.astype(F32)) * skip_scale).astype(BF16) for a, b in zip(h, skip))


def hop(frames, source, target):
    return tuple(sent(f, plane_to_plane(source, target)) for f in frames)


def spread_clips(noisy):
    zlo, core, x = (lax.axis_index(n) for n in ("zlo", "core", "x"))
    clips = noisy.reshape(4, PIX, CH)
    got = []
    for r in range(2):
        clip = lax.dynamic_index_in_dim(clips, 2 * zlo + (r ^ core), 0, keepdims=False)

        def route(sx, sy, sz, sc, r=r):
            hi, lo = sz // 2, sz % 2
            clip = 2 * lo + (r ^ sc)
            return (clip, sy, (2 * sx + hi // 2 - 2 * clip) % NZ, hi % 2) if sy % 2 else None

        got.append(sent(clip, route))
    even = (x ^ core) % 2 == 0
    frames = jnp.where(even, got[0], got[1]), jnp.where(even, got[1], got[0])
    frames = jnp.stack(frames)
    return frames, sent(frames, plane_to_plane(1, 0))


def deliver(h):
    y, zlo, core, x = (lax.axis_index(n) for n in ("y", "zlo", "core", "x"))
    rows = jnp.stack(h).reshape(2, NY, 2, 2, SIDE, CH)
    mine = rows[:, NY - 1]
    for target in range(NY - 1):
        got = sent(rows[:, target], plane_to_plane(NY - 1, target))
        mine = jnp.where(y == target, got, mine)
    def to_owner(sx, sy, sz, sc):
        block = block_of(sx, sz)
        return (block // 2, sy, 2 * (2 * (block % 2) + sc) + sx % 2, sx // 2)

    def other_chip(sx, sy, sz, sc):
        return (sx, sy, sz ^ 1, sc)

    natural = jnp.where(core == 0, mine, mine[::-1])
    held = sent(natural, to_owner)
    got = sent(lax.dynamic_index_in_dim(held, 1 - core, 0, keepdims=False), other_core)
    kept = lax.dynamic_index_in_dim(held, core, 0, keepdims=False)
    by_core = jnp.stack([jnp.where(core == 0, kept, got), jnp.where(core == 0, got, kept)])
    got = sent(lax.dynamic_index_in_dim(by_core, 1 - zlo, 1, keepdims=False), other_chip)
    kept = lax.dynamic_index_in_dim(by_core, zlo, 1, keepdims=False)
    even, odd = jnp.where(zlo == 0, kept, got), jnp.where(zlo == 0, got, kept)
    return jnp.stack([even, odd], axis=1).reshape(4, 1, 2, SIDE, CH)


def put(buffer, piece, *start):
    return lax.dynamic_update_slice(buffer, piece, start)


def gathered(conv_first, conv_second, temporal):
    conv_first = jnp.concatenate([conv_first, temporal[1:2]], axis=0)
    x, zhi, zlo, core = (lax.axis_index(n).astype(jnp.uint32) for n in ("x", "zhi", "zlo", "core"))
    z = 2 * zhi + zlo
    zero = jnp.uint32(0)

    right = sent(conv_first, along(1, 0))
    left = sent(conv_first, along(-1, 0))
    far = sent(right, along(1, 0))
    row = jnp.zeros((10, NX, 16, CH), BF16)
    for piece, offset in ((conv_first, 0), (right, -1), (left, 1), (far, 2)):
        row = put(row, piece.reshape(10, 1, 16, CH), zero, (x + np.uint32(offset % NX)) & np.uint32(NX - 1), zero, zero)

    tail = jnp.concatenate([conv_second, temporal[0:1], temporal[2:3]], axis=0)
    taps = tail.shape[0]
    by_z = [(tail, 0)]
    right = left = tail
    for d in range(1, 5):
        right = sent(right, along(0, 1))
        by_z.append((right, -d))
        if d < 4:
            left = sent(left, along(0, -1))
            by_z.append((left, d))
    tails = jnp.zeros((taps, 2, NZ // 2, 16, CH), BF16)
    for piece, offset in by_z:
        source = (z + np.uint32(offset % NZ)) & np.uint32(NZ - 1)
        tails = put(tails, piece.reshape(taps, 1, 1, 16, CH), zero, source & 1, source >> 1, zero, zero)
    tails, row = lax.optimization_barrier((tails, row))
    second = lax.all_gather(tails, ("x", "core"), axis=0, tiled=False)
    second = second.reshape(NX, 2, taps, 2, NZ // 2, 16, CH)

    pieces = [(row, 0, 0)]
    right = left = row
    for d in range(1, 4):
        right, left = sent(right, along(0, 1)), sent(left, along(0, -1))
        pieces += [(right, -d, 0), (left, d, 0)]
    half = NX // 2
    pieces.append((sent(right[:, :half], along(0, 1)), 4, 0))
    pieces.append((sent(left[:, half:], along(0, -1)), 4, half))
    first = jnp.zeros((10, 2, NX, NZ // 2, 2, 16, CH), BF16)
    for piece, offset, start in pieces:
        source = (z + np.uint32(offset % NZ)) & np.uint32(NZ - 1)
        for block, owner in ((piece, core), (sent(piece, other_core), core ^ 1)):
            block = block.reshape(10, 1, -1, 1, 1, 16, CH)
            at = (zero, source & 1, jnp.uint32(start), source >> 1, owner, zero, zero)
            first = put(first, block, *at)
    return first.reshape(10, 2 * CH, CH), second


def on_device(noisy, conv_first, conv_second, temporal):
    frames, passed = spread_clips(noisy)
    first, second = gathered(conv_first[0], conv_second[0], temporal[0])
    first, frames, passed = lax.optimization_barrier((first, frames, passed))
    e0 = jnp.where(lax.axis_index("y") == 0, passed, frames)
    e0 = e0[0], e0[1]
    middle = first[9]
    core = lax.axis_index("core").astype(jnp.int32).reshape(1)

    def run(e, which):
        return section(e, first, middle, second, core, which)

    e1 = run(e0, 0)
    skip6 = hop(e1, 0, 3)
    e2 = hop(run(e1, 1), 0, 1)
    skip5 = hop(e2, 1, 2)
    e3 = run(e2, 0)
    e4 = hop(joined(run(e3, 1), e3), 1, 2)
    h = run(e4, 0)
    h = hop(run(joined(h, skip5), 1), 2, 3)
    h = run(joined(h, skip6), 0)
    h = run(joined(h, e0), 1)
    return deliver(h)


def solution(mesh):
    fine = Mesh(mesh.devices.reshape(NY, 2, NX, NZ // 2, 2), AXES)
    weight_spec = P(SEGMENT, None, FRAME, None)
    return jax.shard_map(
        on_device,
        mesh=fine,
        in_specs=(P(None, FRAME), weight_spec, weight_spec, weight_spec),
        out_specs=P(None, FRAME, SEGMENT),
        check_vma=False,
    )
```

```python
import functools
import itertools

import jax
import jax.numpy as jnp
import numpy as np
from jax import lax
from jax.experimental import pallas as pl
from jax.experimental.pallas import tpu as pltpu
from jax.sharding import Mesh
from jax.sharding import PartitionSpec as P

skip_scale = 0.7071067811865476
AXES = ("y", "zlo", "x", "zhi", "core")
SEGMENT = ("y", "zlo")
FRAME = ("x", "zhi", "core")
PLANE = ("zlo", "x", "zhi", "core")
NY, NX, NZ = 4, 4, 8
SIDE = 16
CH = 512
PIX = SIDE * SIDE
F32 = jnp.float32
BF16 = jnp.bfloat16


def flat(x, y, z, core):
    return (((y * 2 + z % 2) * 4 + x) * 4 + z // 2) * 2 + core


def sent(value, route):
    pairs = []
    for x, y, z, core in itertools.product(range(NX), range(NY), range(NZ), range(2)):
        target = route(x, y, z, core)
        if target is not None:
            pairs.append((flat(x, y, z, core), flat(*target)))
    return lax.ppermute(value, AXES, pairs)


def block_of(x, z):
    return (z + 2 * x) % NZ


def outward(x, y, z, core):
    step = 2 * core - 1
    return (x, y, (z + step) % NZ, 1 - core) if 0 <= block_of(x, z) + step < NZ else None


def along(dx, dz):
    return lambda x, y, z, core: ((x + dx) % NX, y, (z + dz) % NZ, core)


def other_core(x, y, z, core):
    return (x, y, z, 1 - core)


def plane_to_plane(source, target):
    return lambda x, y, z, core: (x, target, z, core) if y == source else None


def silu(u):
    return u / (1.0 + jnp.exp(-u))


def widen(frame, wide_ref, index):
    full = frame.astype(F32)
    column = lax.broadcasted_iota(jnp.int32, (PIX, CH), 0) % SIDE
    before = jnp.where(column == 0, 0.0, pltpu.roll(full, 1, 0)).astype(BF16)
    after = jnp.where(column == SIDE - 1, 0.0, pltpu.roll(full, PIX - 1, 0)).astype(BF16)
    edge = jnp.zeros((SIDE, 3 * CH), BF16)
    wide_ref[index, 0:SIDE, :] = edge
    wide_ref[index, SIDE + PIX : 2 * SIDE + PIX, :] = edge
    wide_ref[index, SIDE : SIDE + PIX, 0:CH] = before
    wide_ref[index, SIDE : SIDE + PIX, CH : 2 * CH] = frame
    wide_ref[index, SIDE : SIDE + PIX, 2 * CH : 3 * CH] = after


def conv(wide_ref, index, weights_of):
    total = None
    for dy in range(3):
        rows = wide_ref[index, dy * SIDE : dy * SIDE + PIX, :]
        part = jnp.dot(rows, weights_of(dy), preferred_element_type=F32)
        total = part if total is None else total + part
    return total


def stacked_taps(w_ref, which, taps):
    order = itertools.product(taps, range(NX), range(NZ // 2), range(2))
    return jnp.concatenate([w_ref[x, core, t, which, hi] for t, x, hi, core in order], axis=0)


def first_kernel(which, outer_ref, inner_ref, w_ref, outer_out, inner_out, wide_ref):
    widen(outer_ref[...], wide_ref, 0)
    widen(inner_ref[...], wide_ref, 1)

    def weights_of(dy):
        return w_ref[3 * dy : 3 * dy + 3, which * CH : (which + 1) * CH, :].reshape(3 * CH, CH)

    @pl.loop(0, 2)
    def _(i):
        out = silu(conv(wide_ref, i, weights_of)).astype(BF16)

        @pl.when(i == 0)
        def _():
            outer_out[...] = out

        @pl.when(i == 1)
        def _():
            inner_out[...] = out


def second_kernel(which, core_ref, outer_ref, inner_ref, middle_ref, w_ref, acc_ref, wide_ref):
    widen(outer_ref[...], wide_ref, 0)
    widen(inner_ref[...], wide_ref, 1)
    core = core_ref[0]

    @pl.loop(0, 2)
    def _(i):
        total = conv(wide_ref, i, lambda dy: stacked_taps(w_ref, which, range(3 * dy, 3 * dy + 3)))
        own = wide_ref[i, SIDE : SIDE + PIX, CH : 2 * CH]
        middle = middle_ref[which * CH : (which + 1) * CH, :]
        total += jnp.dot(own, middle, preferred_element_type=F32)
        other = wide_ref[1 - i, SIDE : SIDE + PIX, CH : 2 * CH]
        tap = 10 - (core ^ i)
        total += jnp.dot(other, stacked_taps(w_ref, which, [tap]), preferred_element_type=F32)
        acc_ref[i] = total


def last_kernel(which, core_ref, acc_ref, outer_ref, inner_ref, cross_ref, near_ref, w_ref, outer_out, inner_out):
    core = core_ref[0]
    sides = ((outer_ref, cross_ref, outer_out), (inner_ref, near_ref, inner_out))
    for i, (e_ref, beyond_ref, out_ref) in enumerate(sides):
        weights = stacked_taps(w_ref, which, [9 + (core ^ i)])
        total = acc_ref[i] + jnp.dot(beyond_ref[...], weights, preferred_element_type=F32)
        out_ref[...] = (e_ref[...].astype(F32) + silu(total)).astype(BF16)


VM = pl.BlockSpec(memory_space=pltpu.VMEM)
SM = pl.BlockSpec(memory_space=pltpu.SMEM)
FRAME_OUT = jax.ShapeDtypeStruct((PIX, CH), BF16)
WIDE = pltpu.VMEM((2, PIX + 2 * SIDE, 3 * CH), BF16)


def call(kernel, which, in_specs, out_shape, scratch, taps, name):
    return pl.pallas_call(
        functools.partial(kernel, which),
        in_specs=in_specs,
        out_specs=jax.tree.map(lambda _: VM, out_shape),
        out_shape=out_shape,
        scratch_shapes=scratch,
        compiler_params=pltpu.CompilerParams(vmem_limit_bytes=8 << 20),
        cost_estimate=pl.CostEstimate(
            flops=2 * taps * PIX * CH * CH, bytes_accessed=8 * PIX * CH, transcendentals=2 * PIX * CH
        ),
        name=name,
    )


def section(e, first, middle, second, core, which):
    a = call(first_kernel, which, [VM] * 3, (FRAME_OUT,) * 2, [WIDE], 18, "conv_first")(*e, first)
    cross, near = sent(a[0], outward), sent(a[1], other_core)
    acc_shape = jax.ShapeDtypeStruct((2, PIX, CH), F32)
    acc = call(second_kernel, which, [SM] + [VM] * 4, acc_shape, [WIDE], 22, "conv_second")(core, *a, middle, second)
    last = call(last_kernel, which, [SM] + [VM] * 6, (FRAME_OUT,) * 2, [], 2, "halo_and_residual")
    return last(core, acc, *e, cross, near, second)


def joined(h, skip):
    return tuple(((a.astype(F32) + b.astype(F32)) * skip_scale).astype(BF16) for a, b in zip(h, skip))


def hop(frames, source, target):
    return tuple(sent(f, plane_to_plane(source, target)) for f in frames)


def spread_clips(noisy):
    zlo, core, x = (lax.axis_index(n) for n in ("zlo", "core", "x"))
    clips = noisy.reshape(4, PIX, CH)
    got = []
    for r in range(2):
        clip = lax.dynamic_index_in_dim(clips, 2 * zlo + (r ^ core), 0, keepdims=False)

        def route(sx, sy, sz, sc, r=r):
            hi, lo = sz // 2, sz % 2
            clip = 2 * lo + (r ^ sc)
            return (clip, sy, (2 * sx + hi // 2 - 2 * clip) % NZ, hi % 2) if sy == NY - 1 else None

        got.append(sent(clip, route))
    even = (x ^ core) % 2 == 0
    frames = jnp.where(even, got[0], got[1]), jnp.where(even, got[1], got[0])
    frames = jnp.stack(frames)
    return frames, sent(frames, plane_to_plane(NY - 1, 0))


def deliver(h):
    y, zlo, core, x = (lax.axis_index(n) for n in ("y", "zlo", "core", "x"))
    rows = jnp.stack(h).reshape(2, NY, 2, 2, SIDE, CH)
    mine = rows[:, NY - 1]
    for target in range(NY - 1):
        got = sent(rows[:, target], plane_to_plane(NY - 1, target))
        mine = jnp.where(y == target, got, mine)
    def to_owner(sx, sy, sz, sc):
        block = block_of(sx, sz)
        return (block // 2, sy, 2 * (2 * (block % 2) + sc) + sx % 2, sx // 2)

    def other_chip(sx, sy, sz, sc):
        return (sx, sy, sz ^ 1, sc)

    natural = jnp.where(core == 0, mine, mine[::-1])
    held = sent(natural, to_owner)
    got = sent(lax.dynamic_index_in_dim(held, 1 - core, 0, keepdims=False), other_core)
    kept = lax.dynamic_index_in_dim(held, core, 0, keepdims=False)
    by_core = jnp.stack([jnp.where(core == 0, kept, got), jnp.where(core == 0, got, kept)])
    got = sent(lax.dynamic_index_in_dim(by_core, 1 - zlo, 1, keepdims=False), other_chip)
    kept = lax.dynamic_index_in_dim(by_core, zlo, 1, keepdims=False)
    even, odd = jnp.where(zlo == 0, kept, got), jnp.where(zlo == 0, got, kept)
    return jnp.stack([even, odd], axis=1).reshape(4, 1, 2, SIDE, CH)


def put(buffer, piece, *start):
    return lax.dynamic_update_slice(buffer, piece, start)


def gathered(conv_first, conv_second, temporal):
    conv_first = jnp.concatenate([conv_first, temporal[1:2]], axis=0)
    x, zhi, zlo, core = (lax.axis_index(n).astype(jnp.uint32) for n in ("x", "zhi", "zlo", "core"))
    z = 2 * zhi + zlo
    zero = jnp.uint32(0)

    right = sent(conv_first, along(1, 0))
    left = sent(conv_first, along(-1, 0))
    far = sent(right, along(1, 0))
    row = jnp.zeros((10, NX, 16, CH), BF16)
    for piece, offset in ((conv_first, 0), (right, -1), (left, 1), (far, 2)):
        row = put(row, piece.reshape(10, 1, 16, CH), zero, (x + np.uint32(offset % NX)) & np.uint32(NX - 1), zero, zero)

    tail = jnp.concatenate([conv_second, temporal[0:1], temporal[2:3]], axis=0)
    taps = tail.shape[0]
    by_z = [(tail, 0)]
    right = left = tail
    for d in range(1, 5):
        right = sent(right, along(0, 1))
        by_z.append((right, -d))
        if d < 4:
            left = sent(left, along(0, -1))
            by_z.append((left, d))
    tails = jnp.zeros((taps, 2, NZ // 2, 16, CH), BF16)
    for piece, offset in by_z:
        source = (z + np.uint32(offset % NZ)) & np.uint32(NZ - 1)
        tails = put(tails, piece.reshape(taps, 1, 1, 16, CH), zero, source & 1, source >> 1, zero, zero)
    tails, row = lax.optimization_barrier((tails, row))
    second = lax.all_gather(tails, ("x", "core"), axis=0, tiled=False)
    second = second.reshape(NX, 2, taps, 2, NZ // 2, 16, CH)

    pieces = [(row, 0, 0)]
    right = left = row
    for d in range(1, 4):
        right, left = sent(right, along(0, 1)), sent(left, along(0, -1))
        pieces += [(right, -d, 0), (left, d, 0)]
    half = NX // 2
    pieces.append((sent(right[:, :half], along(0, 1)), 4, 0))
    pieces.append((sent(left[:, half:], along(0, -1)), 4, half))
    first = jnp.zeros((10, 2, NX, NZ // 2, 2, 16, CH), BF16)
    for piece, offset, start in pieces:
        source = (z + np.uint32(offset % NZ)) & np.uint32(NZ - 1)
        for block, owner in ((piece, core), (sent(piece, other_core), core ^ 1)):
            block = block.reshape(10, 1, -1, 1, 1, 16, CH)
            at = (zero, source & 1, jnp.uint32(start), source >> 1, owner, zero, zero)
            first = put(first, block, *at)
    return first.reshape(10, 2 * CH, CH), second


def on_device(noisy, conv_first, conv_second, temporal):
    frames, passed = spread_clips(noisy)
    first, second = gathered(conv_first[0], conv_second[0], temporal[0])
    first, frames, passed = lax.optimization_barrier((first, frames, passed))
    e0 = jnp.where(lax.axis_index("y") == 0, passed, frames)
    e0 = e0[0], e0[1]
    middle = first[9]
    core = lax.axis_index("core").astype(jnp.int32).reshape(1)

    def run(e, which):
        return section(e, first, middle, second, core, which)

    e1 = run(e0, 0)
    skip6 = hop(e1, 0, 3)
    e2 = hop(run(e1, 1), 0, 1)
    skip5 = hop(e2, 1, 2)
    e3 = run(e2, 0)
    e4 = hop(joined(run(e3, 1), e3), 1, 2)
    h = run(e4, 0)
    h = hop(run(joined(h, skip5), 1), 2, 3)
    h = run(joined(h, skip6), 0)
    h = run(joined(h, e0), 1)
    return deliver(h)


def solution(mesh):
    fine = Mesh(mesh.devices.reshape(NY, 2, NX, NZ // 2, 2), AXES)
    weight_spec = P(SEGMENT, None, FRAME, None)
    return jax.shard_map(
        on_device,
        mesh=fine,
        in_specs=(P(None, FRAME), weight_spec, weight_spec, weight_spec),
        out_specs=P(None, FRAME, SEGMENT),
        check_vma=False,
    )
```

```python
import functools
import itertools

import jax
import jax.numpy as jnp
import numpy as np
from jax import lax
from jax.experimental import pallas as pl
from jax.experimental.pallas import tpu as pltpu
from jax.sharding import Mesh
from jax.sharding import PartitionSpec as P

skip_scale = 0.7071067811865476
AXES = ("y", "zlo", "x", "zhi", "core")
SEGMENT = ("y", "zlo")
FRAME = ("x", "zhi", "core")
PLANE = ("zlo", "x", "zhi", "core")
NY, NX, NZ = 4, 4, 8
SIDE = 16
CH = 512
LANES = 128
PIX = SIDE * SIDE
F32 = jnp.float32
BF16 = jnp.bfloat16


def flat(x, y, z, core):
    return (((y * 2 + z % 2) * 4 + x) * 4 + z // 2) * 2 + core


def sent(value, route):
    pairs = []
    for x, y, z, core in itertools.product(range(NX), range(NY), range(NZ), range(2)):
        target = route(x, y, z, core)
        if target is not None:
            pairs.append((flat(x, y, z, core), flat(*target)))
    return lax.ppermute(value, AXES, pairs)


def block_of(x, z):
    return (z + 2 * x) % NZ


def outward(x, y, z, core):
    step = 2 * core - 1
    return (x, y, (z + step) % NZ, 1 - core) if 0 <= block_of(x, z) + step < NZ else None


def along(dx, dz):
    return lambda x, y, z, core: ((x + dx) % NX, y, (z + dz) % NZ, core)


def other_core(x, y, z, core):
    return (x, y, z, 1 - core)


def plane_to_plane(source, target):
    return lambda x, y, z, core: (x, target, z, core) if y == source else None


def silu(u):
    return u / (1.0 + jnp.exp(-u))


def widen(frame_ref, wide_ref, index):
    edge = jnp.zeros((SIDE, 3 * CH), BF16)
    wide_ref[index, 0:SIDE, :] = edge
    wide_ref[index, SIDE + PIX : 2 * SIDE + PIX, :] = edge
    column = lax.broadcasted_iota(jnp.int32, (PIX, LANES), 0) % SIDE

    @pl.loop(0, CH // LANES)
    def _(j):
        at = [pl.ds(pl.multiple_of(k * CH + j * LANES, LANES), LANES) for k in range(3)]
        frame = frame_ref[:, at[0]]
        full = frame.astype(F32)
        before = jnp.where(column == 0, 0.0, pltpu.roll(full, 1, 0)).astype(BF16)
        after = jnp.where(column == SIDE - 1, 0.0, pltpu.roll(full, PIX - 1, 0)).astype(BF16)
        for lanes, copy in zip(at, (before, frame, after)):
            wide_ref[index, SIDE : SIDE + PIX, lanes] = copy


def conv(wide_ref, index, weights_of):
    total = None
    for dy in range(3):
        rows = wide_ref[index, dy * SIDE : dy * SIDE + PIX, :]
        part = jnp.dot(rows, weights_of(dy), preferred_element_type=F32)
        total = part if total is None else total + part
    return total


def stacked_taps(w_ref, taps):
    order = itertools.product(taps, range(NX), range(NZ // 2), range(2))
    return jnp.concatenate([w_ref[x, core, t, hi] for t, x, hi, core in order], axis=0)


def first_kernel(which, outer_ref, inner_ref, w_ref, outer_out, inner_out, wide_ref):
    widen(outer_ref, wide_ref, 0)
    widen(inner_ref, wide_ref, 1)

    def weights_of(dy):
        return w_ref[3 * dy : 3 * dy + 3, which * CH : (which + 1) * CH, :].reshape(3 * CH, CH)

    @pl.loop(0, 2)
    def _(i):
        out = silu(conv(wide_ref, i, weights_of)).astype(BF16)

        @pl.when(i == 0)
        def _():
            outer_out[...] = out

        @pl.when(i == 1)
        def _():
            inner_out[...] = out


def second_kernel(which, core_ref, outer_ref, inner_ref, middle_ref, w_ref, acc_ref, wide_ref):
    widen(outer_ref, wide_ref, 0)
    widen(inner_ref, wide_ref, 1)
    core = core_ref[0]

    @pl.loop(0, 2)
    def _(i):
        total = conv(wide_ref, i, lambda dy: stacked_taps(w_ref, range(3 * dy, 3 * dy + 3)))
        own = wide_ref[i, SIDE : SIDE + PIX, CH : 2 * CH]
        middle = middle_ref[which * CH : (which + 1) * CH, :]
        total += jnp.dot(own, middle, preferred_element_type=F32)
        other = wide_ref[1 - i, SIDE : SIDE + PIX, CH : 2 * CH]
        tap = 10 - (core ^ i)
        total += jnp.dot(other, stacked_taps(w_ref, [tap]), preferred_element_type=F32)
        acc_ref[i] = total


def last_kernel(which, core_ref, acc_ref, outer_ref, inner_ref, cross_ref, near_ref, w_ref, outer_out, inner_out):
    core = core_ref[0]
    sides = ((outer_ref, cross_ref, outer_out), (inner_ref, near_ref, inner_out))
    for i, (e_ref, beyond_ref, out_ref) in enumerate(sides):
        weights = stacked_taps(w_ref, [9 + (core ^ i)])
        total = acc_ref[i] + jnp.dot(beyond_ref[...], weights, preferred_element_type=F32)
        out_ref[...] = (e_ref[...].astype(F32) + silu(total)).astype(BF16)


VM = pl.BlockSpec(memory_space=pltpu.VMEM)
SM = pl.BlockSpec(memory_space=pltpu.SMEM)
FRAME_OUT = jax.ShapeDtypeStruct((PIX, CH), BF16)
WIDE = pltpu.VMEM((2, PIX + 2 * SIDE, 3 * CH), BF16)


def call(kernel, which, in_specs, out_shape, scratch, taps, name):
    return pl.pallas_call(
        functools.partial(kernel, which),
        in_specs=in_specs,
        out_specs=jax.tree.map(lambda _: VM, out_shape),
        out_shape=out_shape,
        scratch_shapes=scratch,
        compiler_params=pltpu.CompilerParams(vmem_limit_bytes=8 << 20),
        cost_estimate=pl.CostEstimate(
            flops=2 * taps * PIX * CH * CH, bytes_accessed=8 * PIX * CH, transcendentals=2 * PIX * CH
        ),
        name=name,
    )


def section(e, first, middle, second, core, which):
    a = call(first_kernel, which, [VM] * 3, (FRAME_OUT,) * 2, [WIDE], 18, "conv_first")(*e, first)
    cross, near = sent(a[0], outward), sent(a[1], other_core)
    acc_shape = jax.ShapeDtypeStruct((2, PIX, CH), F32)
    acc = call(second_kernel, which, [SM] + [VM] * 4, acc_shape, [WIDE], 22, "conv_second")(core, *a, middle, second)
    last = call(last_kernel, which, [SM] + [VM] * 6, (FRAME_OUT,) * 2, [], 2, "halo_and_residual")
    return last(core, acc, *e, cross, near, second)


def joined(h, skip):
    return tuple(((a.astype(F32) + b.astype(F32)) * skip_scale).astype(BF16) for a, b in zip(h, skip))


def hop(frames, source, target):
    return tuple(sent(f, plane_to_plane(source, target)) for f in frames)


def spread_clips(noisy):
    zlo, core, x = (lax.axis_index(n) for n in ("zlo", "core", "x"))
    clips = noisy.reshape(4, PIX, CH)
    got = []
    for r in range(2):
        clip = lax.dynamic_index_in_dim(clips, 2 * zlo + (r ^ core), 0, keepdims=False)

        def route(sx, sy, sz, sc, r=r):
            hi, lo = sz // 2, sz % 2
            clip = 2 * lo + (r ^ sc)
            return (clip, sy, (2 * sx + hi // 2 - 2 * clip) % NZ, hi % 2) if sy == NY - 1 else None

        got.append(sent(clip, route))
    even = (x ^ core) % 2 == 0
    frames = jnp.where(even, got[0], got[1]), jnp.where(even, got[1], got[0])
    frames = jnp.stack(frames)
    return frames, sent(frames, plane_to_plane(NY - 1, 0))


def deliver(h):
    y, zlo, core, x = (lax.axis_index(n) for n in ("y", "zlo", "core", "x"))
    rows = jnp.stack(h).reshape(2, NY, 2, 2, SIDE, CH)
    mine = rows[:, NY - 1]
    for target in range(NY - 1):
        got = sent(rows[:, target], plane_to_plane(NY - 1, target))
        mine = jnp.where(y == target, got, mine)
    natural = jnp.where(core == 0, mine, mine[::-1])
    got = []
    for r in range(2):

        def to_owner(sx, sy, sz, sc, r=r):
            block = block_of(sx, sz)
            return (block // 2, sy, 2 * (2 * (block % 2) + sc) + (sx ^ r) % 2, sx // 2)

        message = lax.dynamic_index_in_dim(natural, (x ^ r) % 2, 1, keepdims=False)
        got.append(sent(message, to_owner))
    pair = jnp.stack([jnp.where(zlo == 0, got[0], got[1]), jnp.where(zlo == 0, got[1], got[0])])
    kept = lax.dynamic_index_in_dim(pair, core, 1, keepdims=False)
    swapped = sent(lax.dynamic_index_in_dim(pair, 1 - core, 1, keepdims=False), other_core)
    out = jnp.stack([jnp.where(core == 0, kept, swapped), jnp.where(core == 0, swapped, kept)])
    return out.reshape(4, 1, 2, SIDE, CH)


def put(buffer, piece, *start):
    return lax.dynamic_update_slice(buffer, piece, start)


def gathered(conv_first, conv_second, temporal):
    conv_first = jnp.concatenate([conv_first, temporal[1:2]], axis=0)
    x, zhi, zlo, core = (lax.axis_index(n).astype(jnp.uint32) for n in ("x", "zhi", "zlo", "core"))
    z = 2 * zhi + zlo
    zero = jnp.uint32(0)

    tail = jnp.concatenate([conv_second, temporal[0:1], temporal[2:3]], axis=0)
    taps = tail.shape[0]
    by_z = [(tail, 0)]
    right = left = tail
    for d in range(1, 5):
        right = sent(right, along(0, 1))
        if d == 1:
            right, conv_first = lax.optimization_barrier((right, conv_first))
        by_z.append((right, -d))
        if d < 4:
            left = sent(left, along(0, -1))
            by_z.append((left, d))
    tails = jnp.zeros((taps, 2, NZ // 2, 16, CH), BF16)
    for piece, offset in by_z:
        source = (z + np.uint32(offset % NZ)) & np.uint32(NZ - 1)
        tails = put(tails, piece.reshape(taps, 1, 1, 16, CH), zero, source & 1, source >> 1, zero, zero)
    x_right = sent(conv_first, along(1, 0))
    x_left = sent(conv_first, along(-1, 0))
    far = sent(x_right, along(1, 0))
    row = jnp.zeros((10, NX, 16, CH), BF16)
    for piece, offset in ((conv_first, 0), (x_right, -1), (x_left, 1), (far, 2)):
        row = put(row, piece.reshape(10, 1, 16, CH), zero, (x + np.uint32(offset % NX)) & np.uint32(NX - 1), zero, zero)

    tails, row = lax.optimization_barrier((tails, row))
    second = [
        lax.all_gather(tails[:, parity], ("x", "core"), axis=0, tiled=False).reshape(NX, 2, taps, NZ // 2, 16, CH)
        for parity in range(2)
    ]

    pieces = [(row, 0, 0)]
    right = left = row
    for d in range(1, 4):
        right, left = sent(right, along(0, 1)), sent(left, along(0, -1))
        pieces += [(right, -d, 0), (left, d, 0)]
    half = NX // 2
    pieces.append((sent(right[:, :half], along(0, 1)), 4, 0))
    pieces.append((sent(left[:, half:], along(0, -1)), 4, half))
    first = jnp.zeros((10, 2, NX, NZ // 2, 2, 16, CH), BF16)
    for piece, offset, start in pieces:
        source = (z + np.uint32(offset % NZ)) & np.uint32(NZ - 1)
        for block, owner in ((piece, core), (sent(piece, other_core), core ^ 1)):
            block = block.reshape(10, 1, -1, 1, 1, 16, CH)
            at = (zero, source & 1, jnp.uint32(start), source >> 1, owner, zero, zero)
            first = put(first, block, *at)
    return first.reshape(10, 2 * CH, CH), second


def on_device(noisy, conv_first, conv_second, temporal):
    frames, passed = spread_clips(noisy)
    first, second = gathered(conv_first[0], conv_second[0], temporal[0])
    first, frames, passed = lax.optimization_barrier((first, frames, passed))
    e0 = jnp.where(lax.axis_index("y") == 0, passed, frames)
    e0 = e0[0], e0[1]
    middle = first[9]
    core = lax.axis_index("core").astype(jnp.int32).reshape(1)

    def run(e, which):
        return section(e, first, middle, second[which], core, which)

    e1 = run(e0, 0)
    skip6 = hop(e1, 0, 3)
    e2 = hop(run(e1, 1), 0, 1)
    skip5 = hop(e2, 1, 2)
    e3 = run(e2, 0)
    e4 = hop(joined(run(e3, 1), e3), 1, 2)
    h = run(e4, 0)
    h = hop(run(joined(h, skip5), 1), 2, 3)
    h = run(joined(h, skip6), 0)
    h = run(joined(h, e0), 1)
    return deliver(h)


def solution(mesh):
    fine = Mesh(mesh.devices.reshape(NY, 2, NX, NZ // 2, 2), AXES)
    weight_spec = P(SEGMENT, None, FRAME, None)
    return jax.shard_map(
        on_device,
        mesh=fine,
        in_specs=(P(None, FRAME), weight_spec, weight_spec, weight_spec),
        out_specs=P(None, FRAME, SEGMENT),
        check_vma=False,
    )
```

```python
import functools
import itertools

import jax
import jax.numpy as jnp
import numpy as np
from jax import lax
from jax.experimental import pallas as pl
from jax.experimental.pallas import tpu as pltpu
from jax.sharding import Mesh
from jax.sharding import PartitionSpec as P

skip_scale = 0.7071067811865476
AXES = ("y", "zlo", "x", "zhi", "core")
SEGMENT = ("y", "zlo")
FRAME = ("x", "zhi", "core")
PLANE = ("zlo", "x", "zhi", "core")
NY, NX, NZ = 4, 4, 8
SIDE = 16
CH = 512
HALF = 256
PIX = SIDE * SIDE
F32 = jnp.float32
BF16 = jnp.bfloat16


def flat(x, y, z, core):
    return (((y * 2 + z % 2) * 4 + x) * 4 + z // 2) * 2 + core


def sent(value, route):
    pairs = []
    for x, y, z, core in itertools.product(range(NX), range(NY), range(NZ), range(2)):
        target = route(x, y, z, core)
        if target is not None:
            pairs.append((flat(x, y, z, core), flat(*target)))
    return lax.ppermute(value, AXES, pairs)


def block_of(x, z):
    return (z + 2 * x) % NZ


def outward(x, y, z, core):
    step = 2 * core - 1
    return (x, y, (z + step) % NZ, 1 - core) if 0 <= block_of(x, z) + step < NZ else None


def along(dx, dz):
    return lambda x, y, z, core: ((x + dx) % NX, y, (z + dz) % NZ, core)


def other_core(x, y, z, core):
    return (x, y, z, 1 - core)


def plane_to_plane(source, target):
    return lambda x, y, z, core: (x, target, z, core) if y == source else None


def silu(u):
    return u / (1.0 + jnp.exp(-u))


def conv(frame, wide_ref, weights_of):
    full = frame.astype(F32)
    column = lax.broadcasted_iota(jnp.int32, (PIX, CH), 0) % SIDE
    before = jnp.where(column == 0, 0.0, pltpu.roll(full, 1, 0)).astype(BF16)
    after = jnp.where(column == SIDE - 1, 0.0, pltpu.roll(full, PIX - 1, 0)).astype(BF16)
    edge = jnp.zeros((SIDE, 3 * CH), BF16)
    wide_ref[0:SIDE, :] = edge
    wide_ref[SIDE + PIX : 2 * SIDE + PIX, :] = edge
    wide_ref[SIDE : SIDE + PIX, 0:CH] = before
    wide_ref[SIDE : SIDE + PIX, CH : 2 * CH] = frame
    wide_ref[SIDE : SIDE + PIX, 2 * CH : 3 * CH] = after
    parts = []
    for n in range(0, CH, HALF):
        total = None
        for dy in range(3):
            rows = wide_ref[dy * SIDE : dy * SIDE + PIX, :]
            part = jnp.dot(rows, weights_of(dy, slice(n, n + HALF)), preferred_element_type=F32)
            total = part if total is None else total + part
        parts.append((slice(n, n + HALF), total))
    return parts


def stacked_taps(w_ref, which, taps, lanes=slice(None)):
    order = itertools.product(taps, range(NX), range(NZ // 2), range(2))
    return jnp.concatenate([w_ref[x, core, t, which, hi, :, lanes] for t, x, hi, core in order], axis=0)


def first_kernel(which, e_ref, w_ref, out_ref, wide_ref):
    def weights_of(dy, lanes):
        return w_ref[3 * dy : 3 * dy + 3, which * CH : (which + 1) * CH, lanes].reshape(3 * CH, HALF)

    for lanes, total in conv(e_ref[...], wide_ref, weights_of):
        out_ref[:, lanes] = silu(total).astype(BF16)


def second_kernel(which, role, core_ref, own_ref, other_ref, middle_ref, w_ref, acc_ref, wide_ref):
    tap = 10 - (core_ref[0] ^ role)

    def weights_of(dy, lanes):
        return stacked_taps(w_ref, which, range(3 * dy, 3 * dy + 3), lanes)

    for lanes, total in conv(own_ref[...], wide_ref, weights_of):
        middle = middle_ref[which * CH : (which + 1) * CH, lanes]
        total += jnp.dot(own_ref[...], middle, preferred_element_type=F32)
        total += jnp.dot(other_ref[...], stacked_taps(w_ref, which, [tap], lanes), preferred_element_type=F32)
        acc_ref[:, lanes] = total


def last_kernel(which, role, core_ref, acc_ref, e_ref, beyond_ref, w_ref, out_ref):
    weights = stacked_taps(w_ref, which, [9 + (core_ref[0] ^ role)])
    total = acc_ref[...] + jnp.dot(beyond_ref[...], weights, preferred_element_type=F32)
    out_ref[...] = (e_ref[...].astype(F32) + silu(total)).astype(BF16)


VM = pl.BlockSpec(memory_space=pltpu.VMEM)
SM = pl.BlockSpec(memory_space=pltpu.SMEM)
FRAME_OUT = jax.ShapeDtypeStruct((PIX, CH), BF16)
FRAME_SUM = jax.ShapeDtypeStruct((PIX, CH), F32)
WIDE = pltpu.VMEM((PIX + 2 * SIDE, 3 * CH), BF16)


def call(kernel, in_specs, out_shape, scratch, taps, name):
    return pl.pallas_call(
        kernel,
        in_specs=in_specs,
        out_specs=VM,
        out_shape=out_shape,
        scratch_shapes=scratch,
        compiler_params=pltpu.CompilerParams(vmem_limit_bytes=8 << 20),
        cost_estimate=pl.CostEstimate(
            flops=2 * taps * PIX * CH * CH, bytes_accessed=4 * PIX * CH, transcendentals=PIX * CH
        ),
        name=name,
    )


def section(e, first, middle, second, core, which):
    one = call(functools.partial(first_kernel, which), [VM] * 2, FRAME_OUT, [WIDE], 9, "conv_first")
    a_outer = one(e[0], first)
    cross = sent(a_outer, outward)
    a_inner = one(e[1], first)
    near = sent(a_inner, other_core)
    out = []
    for role, (own, other, beyond) in enumerate(((a_outer, a_inner, cross), (a_inner, a_outer, near))):
        two = functools.partial(second_kernel, which, role)
        acc = call(two, [SM] + [VM] * 4, FRAME_SUM, [WIDE], 11, "conv_second")(core, own, other, middle, second)
        last = functools.partial(last_kernel, which, role)
        out.append(call(last, [SM] + [VM] * 4, FRAME_OUT, [], 1, "halo_and_residual")(core, acc, e[role], beyond, second))
    return tuple(out)


def joined(h, skip):
    return tuple(((a.astype(F32) + b.astype(F32)) * skip_scale).astype(BF16) for a, b in zip(h, skip))


def hop(frames, source, target):
    return tuple(sent(f, plane_to_plane(source, target)) for f in frames)


def spread_clips(noisy):
    zlo, core, x = (lax.axis_index(n) for n in ("zlo", "core", "x"))
    clips = noisy.reshape(4, PIX, CH)
    got = []
    for r in range(2):
        clip = lax.dynamic_index_in_dim(clips, 2 * zlo + (r ^ core), 0, keepdims=False)

        def route(sx, sy, sz, sc, r=r):
            hi, lo = sz // 2, sz % 2
            clip = 2 * lo + (r ^ sc)
            return (clip, sy, (2 * sx + hi // 2 - 2 * clip) % NZ, hi % 2) if sy == NY - 1 else None

        got.append(sent(clip, route))
    even = (x ^ core) % 2 == 0
    frames = jnp.where(even, got[0], got[1]), jnp.where(even, got[1], got[0])
    frames = jnp.stack(frames)
    return frames, sent(frames, plane_to_plane(NY - 1, 0))


def deliver(h):
    y, zlo, core, x = (lax.axis_index(n) for n in ("y", "zlo", "core", "x"))
    rows = jnp.stack(h).reshape(2, NY, 2, 2, SIDE, CH)
    mine = rows[:, NY - 1]
    for target in range(NY - 1):
        got = sent(rows[:, target], plane_to_plane(NY - 1, target))
        mine = jnp.where(y == target, got, mine)
    def to_owner(sx, sy, sz, sc):
        block = block_of(sx, sz)
        return (block // 2, sy, 2 * (2 * (block % 2) + sc) + sx % 2, sx // 2)

    def other_chip(sx, sy, sz, sc):
        return (sx, sy, sz ^ 1, sc)

    natural = jnp.where(core == 0, mine, mine[::-1])
    held = sent(natural, to_owner)
    got = sent(lax.dynamic_index_in_dim(held, 1 - core, 0, keepdims=False), other_core)
    kept = lax.dynamic_index_in_dim(held, core, 0, keepdims=False)
    by_core = jnp.stack([jnp.where(core == 0, kept, got), jnp.where(core == 0, got, kept)])
    got = sent(lax.dynamic_index_in_dim(by_core, 1 - zlo, 1, keepdims=False), other_chip)
    kept = lax.dynamic_index_in_dim(by_core, zlo, 1, keepdims=False)
    even, odd = jnp.where(zlo == 0, kept, got), jnp.where(zlo == 0, got, kept)
    return jnp.stack([even, odd], axis=1).reshape(4, 1, 2, SIDE, CH)


def put(buffer, piece, *start):
    return lax.dynamic_update_slice(buffer, piece, start)


def gathered(conv_first, conv_second, temporal):
    conv_first = jnp.concatenate([conv_first, temporal[1:2]], axis=0)
    x, zhi, zlo, core = (lax.axis_index(n).astype(jnp.uint32) for n in ("x", "zhi", "zlo", "core"))
    z = 2 * zhi + zlo
    zero = jnp.uint32(0)

    right = sent(conv_first, along(1, 0))
    left = sent(conv_first, along(-1, 0))
    far = sent(right, along(1, 0))
    row = jnp.zeros((10, NX, 16, CH), BF16)
    for piece, offset in ((conv_first, 0), (right, -1), (left, 1), (far, 2)):
        row = put(row, piece.reshape(10, 1, 16, CH), zero, (x + np.uint32(offset % NX)) & np.uint32(NX - 1), zero, zero)

    tail = jnp.concatenate([conv_second, temporal[0:1], temporal[2:3]], axis=0)
    taps = tail.shape[0]
    by_z = [(tail, 0)]
    right = left = tail
    for d in range(1, 5):
        right = sent(right, along(0, 1))
        by_z.append((right, -d))
        if d < 4:
            left = sent(left, along(0, -1))
            by_z.append((left, d))
    tails = jnp.zeros((taps, 2, NZ // 2, 16, CH), BF16)
    for piece, offset in by_z:
        source = (z + np.uint32(offset % NZ)) & np.uint32(NZ - 1)
        tails = put(tails, piece.reshape(taps, 1, 1, 16, CH), zero, source & 1, source >> 1, zero, zero)
    tails, row = lax.optimization_barrier((tails, row))
    second = lax.all_gather(tails, ("x", "core"), axis=0, tiled=False)
    second = second.reshape(NX, 2, taps, 2, NZ // 2, 16, CH)

    pieces = [(row, 0, 0)]
    right = left = row
    for d in range(1, 4):
        right, left = sent(right, along(0, 1)), sent(left, along(0, -1))
        pieces += [(right, -d, 0), (left, d, 0)]
    half = NX // 2
    pieces.append((sent(right[:, :half], along(0, 1)), 4, 0))
    pieces.append((sent(left[:, half:], along(0, -1)), 4, half))
    first = jnp.zeros((10, 2, NX, NZ // 2, 2, 16, CH), BF16)
    for piece, offset, start in pieces:
        source = (z + np.uint32(offset % NZ)) & np.uint32(NZ - 1)
        for block, owner in ((piece, core), (sent(piece, other_core), core ^ 1)):
            block = block.reshape(10, 1, -1, 1, 1, 16, CH)
            at = (zero, source & 1, jnp.uint32(start), source >> 1, owner, zero, zero)
            first = put(first, block, *at)
    return first.reshape(10, 2 * CH, CH), second


def on_device(noisy, conv_first, conv_second, temporal):
    frames, passed = spread_clips(noisy)
    first, second = gathered(conv_first[0], conv_second[0], temporal[0])
    first, frames, passed = lax.optimization_barrier((first, frames, passed))
    e0 = jnp.where(lax.axis_index("y") == 0, passed, frames)
    e0 = e0[0], e0[1]
    middle = first[9]
    core = lax.axis_index("core").astype(jnp.int32).reshape(1)

    def run(e, which):
        return section(e, first, middle, second, core, which)

    e1 = run(e0, 0)
    skip6 = hop(e1, 0, 3)
    e2 = hop(run(e1, 1), 0, 1)
    skip5 = hop(e2, 1, 2)
    e3 = run(e2, 0)
    e4 = hop(joined(run(e3, 1), e3), 1, 2)
    h = run(e4, 0)
    h = hop(run(joined(h, skip5), 1), 2, 3)
    h = run(joined(h, skip6), 0)
    h = run(joined(h, e0), 1)
    return deliver(h)


def solution(mesh):
    fine = Mesh(mesh.devices.reshape(NY, 2, NX, NZ // 2, 2), AXES)
    weight_spec = P(SEGMENT, None, FRAME, None)
    return jax.shard_map(
        on_device,
        mesh=fine,
        in_specs=(P(None, FRAME), weight_spec, weight_spec, weight_spec),
        out_specs=P(None, FRAME, SEGMENT),
        check_vma=False,
    )
```

```python
import functools
import itertools

import jax
import jax.numpy as jnp
import numpy as np
from jax import lax
from jax.experimental import pallas as pl
from jax.experimental.pallas import tpu as pltpu
from jax.sharding import Mesh
from jax.sharding import PartitionSpec as P

skip_scale = 0.7071067811865476
AXES = ("y", "zlo", "x", "zhi", "core")
SEGMENT = ("y", "zlo")
FRAME = ("x", "zhi", "core")
PLANE = ("zlo", "x", "zhi", "core")
NY, NX, NZ = 4, 4, 8
SIDE = 16
CH = 512
HALF = 256
PIX = SIDE * SIDE
F32 = jnp.float32
BF16 = jnp.bfloat16


def flat(x, y, z, core):
    return (((y * 2 + z % 2) * 4 + x) * 4 + z // 2) * 2 + core


def sent(value, route):
    pairs = []
    for x, y, z, core in itertools.product(range(NX), range(NY), range(NZ), range(2)):
        target = route(x, y, z, core)
        if target is not None:
            pairs.append((flat(x, y, z, core), flat(*target)))
    return lax.ppermute(value, AXES, pairs)


def block_of(x, z):
    return (z + 2 * x) % NZ


def outward(x, y, z, core):
    step = 2 * core - 1
    return (x, y, (z + step) % NZ, 1 - core) if 0 <= block_of(x, z) + step < NZ else None


def along(dx, dz):
    return lambda x, y, z, core: ((x + dx) % NX, y, (z + dz) % NZ, core)


def other_core(x, y, z, core):
    return (x, y, z, 1 - core)


def plane_to_plane(source, target):
    return lambda x, y, z, core: (x, target, z, core) if y == source else None


def silu(u):
    return u / (1.0 + jnp.exp(-u))


def conv(frame, wide_ref, weights_of):
    full = frame.astype(F32)
    column = lax.broadcasted_iota(jnp.int32, (PIX, CH), 0) % SIDE
    before = jnp.where(column == 0, 0.0, pltpu.roll(full, 1, 0)).astype(BF16)
    after = jnp.where(column == SIDE - 1, 0.0, pltpu.roll(full, PIX - 1, 0)).astype(BF16)
    edge = jnp.zeros((SIDE, 3 * CH), BF16)
    wide_ref[0:SIDE, :] = edge
    wide_ref[SIDE + PIX : 2 * SIDE + PIX, :] = edge
    wide_ref[SIDE : SIDE + PIX, 0:CH] = before
    wide_ref[SIDE : SIDE + PIX, CH : 2 * CH] = frame
    wide_ref[SIDE : SIDE + PIX, 2 * CH : 3 * CH] = after
    parts = []
    for n in range(0, CH, HALF):
        total = None
        for dy in range(3):
            rows = wide_ref[dy * SIDE : dy * SIDE + PIX, :]
            part = jnp.dot(rows, weights_of(dy, slice(n, n + HALF)), preferred_element_type=F32)
            total = part if total is None else total + part
        parts.append((slice(n, n + HALF), total))
    return parts


def stacked_taps(w_ref, which, taps, lanes=slice(None)):
    order = itertools.product(taps, range(NX), range(NZ // 2), range(2))
    return jnp.concatenate([w_ref[x, core, t, which, hi, :, lanes] for t, x, hi, core in order], axis=0)


def first_kernel(which, e_ref, w_ref, out_ref, wide_ref):
    def weights_of(dy, lanes):
        return w_ref[3 * dy : 3 * dy + 3, which * CH : (which + 1) * CH, lanes].reshape(3 * CH, HALF)

    for lanes, total in conv(e_ref[...], wide_ref, weights_of):
        out_ref[:, lanes] = silu(total).astype(BF16)


def second_kernel(which, role, core_ref, own_ref, other_ref, middle_ref, w_ref, acc_ref, wide_ref):
    tap = 10 - (core_ref[0] ^ role)

    def weights_of(dy, lanes):
        return stacked_taps(w_ref, which, range(3 * dy, 3 * dy + 3), lanes)

    for lanes, total in conv(own_ref[...], wide_ref, weights_of):
        middle = middle_ref[which * CH : (which + 1) * CH, lanes]
        total += jnp.dot(own_ref[...], middle, preferred_element_type=F32)
        total += jnp.dot(other_ref[...], stacked_taps(w_ref, which, [tap], lanes), preferred_element_type=F32)
        acc_ref[:, lanes] = total


def last_kernel(which, role, core_ref, acc_ref, e_ref, beyond_ref, w_ref, out_ref):
    weights = stacked_taps(w_ref, which, [9 + (core_ref[0] ^ role)])
    total = acc_ref[...] + jnp.dot(beyond_ref[...], weights, preferred_element_type=F32)
    out_ref[...] = (e_ref[...].astype(F32) + silu(total)).astype(BF16)


VM = pl.BlockSpec(memory_space=pltpu.VMEM)
SM = pl.BlockSpec(memory_space=pltpu.SMEM)
FRAME_OUT = jax.ShapeDtypeStruct((PIX, CH), BF16)
FRAME_SUM = jax.ShapeDtypeStruct((PIX, CH), F32)
WIDE = pltpu.VMEM((PIX + 2 * SIDE, 3 * CH), BF16)


def call(kernel, in_specs, out_shape, scratch, taps, name):
    return pl.pallas_call(
        kernel,
        in_specs=in_specs,
        out_specs=VM,
        out_shape=out_shape,
        scratch_shapes=scratch,
        compiler_params=pltpu.CompilerParams(vmem_limit_bytes=8 << 20),
        cost_estimate=pl.CostEstimate(
            flops=2 * taps * PIX * CH * CH, bytes_accessed=4 * PIX * CH, transcendentals=PIX * CH
        ),
        name=name,
    )


def section(e, first, middle, second, core, which):
    one = call(functools.partial(first_kernel, which), [VM] * 2, FRAME_OUT, [WIDE], 9, "conv_first")
    a_outer = one(e[0], first)
    cross = sent(a_outer, outward)
    a_inner = one(e[1], first)
    near = sent(a_inner, other_core)
    out = []
    for role, (own, other, beyond) in enumerate(((a_outer, a_inner, cross), (a_inner, a_outer, near))):
        two = functools.partial(second_kernel, which, role)
        acc = call(two, [SM] + [VM] * 4, FRAME_SUM, [WIDE], 11, "conv_second")(core, own, other, middle, second)
        last = functools.partial(last_kernel, which, role)
        out.append(call(last, [SM] + [VM] * 4, FRAME_OUT, [], 1, "halo_and_residual")(core, acc, e[role], beyond, second))
    return tuple(out)


def joined(h, skip):
    return tuple(((a.astype(F32) + b.astype(F32)) * skip_scale).astype(BF16) for a, b in zip(h, skip))


def hop(frames, source, target):
    return tuple(sent(f, plane_to_plane(source, target)) for f in frames)


def spread_clips(noisy):
    zlo, core, x = (lax.axis_index(n) for n in ("zlo", "core", "x"))
    clips = noisy.reshape(4, PIX, CH)
    got = []
    for r in range(2):
        clip = lax.dynamic_index_in_dim(clips, 2 * zlo + (r ^ core), 0, keepdims=False)

        def route(sx, sy, sz, sc, r=r):
            hi, lo = sz // 2, sz % 2
            clip = 2 * lo + (r ^ sc)
            return (clip, sy, (2 * sx + hi // 2 - 2 * clip) % NZ, hi % 2) if sy == NY - 1 else None

        got.append(sent(clip, route))
    even = (x ^ core) % 2 == 0
    frames = jnp.where(even, got[0], got[1]), jnp.where(even, got[1], got[0])
    frames = jnp.stack(frames)
    return frames, sent(frames, plane_to_plane(NY - 1, 0))


def deliver(h):
    y, zlo, core, x = (lax.axis_index(n) for n in ("y", "zlo", "core", "x"))
    rows = jnp.stack(h).reshape(2, NY, 2, 2, SIDE, CH)
    mine = rows[:, NY - 1]
    for target in range(NY - 1):
        got = sent(rows[:, target], plane_to_plane(NY - 1, target))
        mine = jnp.where(y == target, got, mine)
    def to_owner(sx, sy, sz, sc):
        block = block_of(sx, sz)
        return (block // 2, sy, 2 * (2 * (block % 2) + sc) + sx % 2, sx // 2)

    def other_chip(sx, sy, sz, sc):
        return (sx, sy, sz ^ 1, sc)

    natural = jnp.where(core == 0, mine, mine[::-1])
    held = sent(natural, to_owner)
    got = sent(lax.dynamic_index_in_dim(held, 1 - core, 0, keepdims=False), other_core)
    kept = lax.dynamic_index_in_dim(held, core, 0, keepdims=False)
    by_core = jnp.stack([jnp.where(core == 0, kept, got), jnp.where(core == 0, got, kept)])
    got = sent(lax.dynamic_index_in_dim(by_core, 1 - zlo, 1, keepdims=False), other_chip)
    kept = lax.dynamic_index_in_dim(by_core, zlo, 1, keepdims=False)
    even, odd = jnp.where(zlo == 0, kept, got), jnp.where(zlo == 0, got, kept)
    return jnp.stack([even, odd], axis=1).reshape(4, 1, 2, SIDE, CH)


def put(buffer, piece, *start):
    return lax.dynamic_update_slice(buffer, piece, start)


def gathered(conv_first, conv_second, temporal):
    conv_first = jnp.concatenate([conv_first, temporal[1:2]], axis=0)
    x, zhi, zlo, core = (lax.axis_index(n).astype(jnp.uint32) for n in ("x", "zhi", "zlo", "core"))
    z = 2 * zhi + zlo
    zero = jnp.uint32(0)

    tail = jnp.concatenate([conv_second, temporal[0:1], temporal[2:3]], axis=0)
    taps = tail.shape[0]
    by_z = [(tail, 0)]
    right = left = tail
    for d in range(1, 5):
        right = sent(right, along(0, 1))
        if d == 2:
            right, conv_first = lax.optimization_barrier((right, conv_first))
        by_z.append((right, -d))
        if d < 4:
            left = sent(left, along(0, -1))
            by_z.append((left, d))
    tails = jnp.zeros((taps, 2, NZ // 2, 16, CH), BF16)
    for piece, offset in by_z:
        source = (z + np.uint32(offset % NZ)) & np.uint32(NZ - 1)
        tails = put(tails, piece.reshape(taps, 1, 1, 16, CH), zero, source & 1, source >> 1, zero, zero)
    x_right = sent(conv_first, along(1, 0))
    x_left = sent(conv_first, along(-1, 0))
    far = sent(x_right, along(1, 0))
    row = jnp.zeros((10, NX, 16, CH), BF16)
    for piece, offset in ((conv_first, 0), (x_right, -1), (x_left, 1), (far, 2)):
        row = put(row, piece.reshape(10, 1, 16, CH), zero, (x + np.uint32(offset % NX)) & np.uint32(NX - 1), zero, zero)

    tails, row = lax.optimization_barrier((tails, row))
    second = lax.all_gather(tails, ("x", "core"), axis=0, tiled=False)
    second = second.reshape(NX, 2, taps, 2, NZ // 2, 16, CH)

    pieces = [(row, 0, 0)]
    right = left = row
    for d in range(1, 4):
        right, left = sent(right, along(0, 1)), sent(left, along(0, -1))
        pieces += [(right, -d, 0), (left, d, 0)]
    half = NX // 2
    pieces.append((sent(right[:, :half], along(0, 1)), 4, 0))
    pieces.append((sent(left[:, half:], along(0, -1)), 4, half))
    first = jnp.zeros((10, 2, NX, NZ // 2, 2, 16, CH), BF16)
    for piece, offset, start in pieces:
        source = (z + np.uint32(offset % NZ)) & np.uint32(NZ - 1)
        for block, owner in ((piece, core), (sent(piece, other_core), core ^ 1)):
            block = block.reshape(10, 1, -1, 1, 1, 16, CH)
            at = (zero, source & 1, jnp.uint32(start), source >> 1, owner, zero, zero)
            first = put(first, block, *at)
    return first.reshape(10, 2 * CH, CH), second


def on_device(noisy, conv_first, conv_second, temporal):
    frames, passed = spread_clips(noisy)
    first, second = gathered(conv_first[0], conv_second[0], temporal[0])
    first, frames, passed = lax.optimization_barrier((first, frames, passed))
    e0 = jnp.where(lax.axis_index("y") == 0, passed, frames)
    e0 = e0[0], e0[1]
    middle = first[9]
    core = lax.axis_index("core").astype(jnp.int32).reshape(1)

    def run(e, which):
        return section(e, first, middle, second, core, which)

    e1 = run(e0, 0)
    skip6 = hop(e1, 0, 3)
    e2 = hop(run(e1, 1), 0, 1)
    skip5 = hop(e2, 1, 2)
    e3 = run(e2, 0)
    e4 = hop(joined(run(e3, 1), e3), 1, 2)
    h = run(e4, 0)
    h = hop(run(joined(h, skip5), 1), 2, 3)
    h = run(joined(h, skip6), 0)
    h = run(joined(h, e0), 1)
    return deliver(h)


def solution(mesh):
    fine = Mesh(mesh.devices.reshape(NY, 2, NX, NZ // 2, 2), AXES)
    weight_spec = P(SEGMENT, None, FRAME, None)
    return jax.shard_map(
        on_device,
        mesh=fine,
        in_specs=(P(None, FRAME), weight_spec, weight_spec, weight_spec),
        out_specs=P(None, FRAME, SEGMENT),
        check_vma=False,
    )
```

```python
import functools
import itertools

import jax
import jax.numpy as jnp
import numpy as np
from jax import lax
from jax.experimental import pallas as pl
from jax.experimental.pallas import tpu as pltpu
from jax.sharding import Mesh
from jax.sharding import PartitionSpec as P

skip_scale = 0.7071067811865476
AXES = ("y", "zlo", "x", "zhi", "core")
SEGMENT = ("y", "zlo")
FRAME = ("x", "zhi", "core")
PLANE = ("zlo", "x", "zhi", "core")
NY, NX, NZ = 4, 4, 8
SIDE = 16
CH = 512
HALF = 256
PIX = SIDE * SIDE
F32 = jnp.float32
BF16 = jnp.bfloat16


def flat(x, y, z, core):
    return (((y * 2 + z % 2) * 4 + x) * 4 + z // 2) * 2 + core


def sent(value, route):
    pairs = []
    for x, y, z, core in itertools.product(range(NX), range(NY), range(NZ), range(2)):
        target = route(x, y, z, core)
        if target is not None:
            pairs.append((flat(x, y, z, core), flat(*target)))
    return lax.ppermute(value, AXES, pairs)


def block_of(x, z):
    return (z + 2 * x) % NZ


def outward(x, y, z, core):
    step = 2 * core - 1
    return (x, y, (z + step) % NZ, 1 - core) if 0 <= block_of(x, z) + step < NZ else None


def along(dx, dz):
    return lambda x, y, z, core: ((x + dx) % NX, y, (z + dz) % NZ, core)


def other_core(x, y, z, core):
    return (x, y, z, 1 - core)


def plane_to_plane(source, target):
    return lambda x, y, z, core: (x, target, z, core) if y == source else None


def silu(u):
    return u / (1.0 + jnp.exp(-u))


def conv(frame, wide_ref, weights_of):
    full = frame.astype(F32)
    column = lax.broadcasted_iota(jnp.int32, (PIX, CH), 0) % SIDE
    before = jnp.where(column == 0, 0.0, pltpu.roll(full, 1, 0)).astype(BF16)
    after = jnp.where(column == SIDE - 1, 0.0, pltpu.roll(full, PIX - 1, 0)).astype(BF16)
    edge = jnp.zeros((SIDE, 3 * CH), BF16)
    wide_ref[0:SIDE, :] = edge
    wide_ref[SIDE + PIX : 2 * SIDE + PIX, :] = edge
    wide_ref[SIDE : SIDE + PIX, 0:CH] = before
    wide_ref[SIDE : SIDE + PIX, CH : 2 * CH] = frame
    wide_ref[SIDE : SIDE + PIX, 2 * CH : 3 * CH] = after
    parts = []
    for n in range(0, CH, HALF):
        total = None
        for dy in range(3):
            rows = wide_ref[dy * SIDE : dy * SIDE + PIX, :]
            part = jnp.dot(rows, weights_of(dy, slice(n, n + HALF)), preferred_element_type=F32)
            total = part if total is None else total + part
        parts.append((slice(n, n + HALF), total))
    return parts


def stacked_taps(w_ref, which, taps, lanes=slice(None)):
    order = itertools.product(taps, range(NX), range(NZ // 2), range(2))
    return jnp.concatenate([w_ref[x, core, t, which, hi, :, lanes] for t, x, hi, core in order], axis=0)


def first_kernel(which, e_ref, w_ref, out_ref, wide_ref):
    def weights_of(dy, lanes):
        return w_ref[3 * dy : 3 * dy + 3, which * CH : (which + 1) * CH, lanes].reshape(3 * CH, HALF)

    for lanes, total in conv(e_ref[...], wide_ref, weights_of):
        out_ref[:, lanes] = silu(total).astype(BF16)


def second_kernel(which, role, core_ref, own_ref, other_ref, middle_ref, w_ref, acc_ref, wide_ref):
    tap = 10 - (core_ref[0] ^ role)

    def weights_of(dy, lanes):
        return stacked_taps(w_ref, which, range(3 * dy, 3 * dy + 3), lanes)

    for lanes, total in conv(own_ref[...], wide_ref, weights_of):
        middle = middle_ref[which * CH : (which + 1) * CH, lanes]
        total += jnp.dot(own_ref[...], middle, preferred_element_type=F32)
        total += jnp.dot(other_ref[...], stacked_taps(w_ref, which, [tap], lanes), preferred_element_type=F32)
        acc_ref[:, lanes] = total


def last_kernel(which, role, core_ref, acc_ref, e_ref, beyond_ref, w_ref, out_ref):
    weights = stacked_taps(w_ref, which, [9 + (core_ref[0] ^ role)])
    total = acc_ref[...] + jnp.dot(beyond_ref[...], weights, preferred_element_type=F32)
    out_ref[...] = (e_ref[...].astype(F32) + silu(total)).astype(BF16)


VM = pl.BlockSpec(memory_space=pltpu.VMEM)
SM = pl.BlockSpec(memory_space=pltpu.SMEM)
FRAME_OUT = jax.ShapeDtypeStruct((PIX, CH), BF16)
FRAME_SUM = jax.ShapeDtypeStruct((PIX, CH), F32)
WIDE = pltpu.VMEM((PIX + 2 * SIDE, 3 * CH), BF16)


def call(kernel, in_specs, out_shape, scratch, taps, name):
    return pl.pallas_call(
        kernel,
        in_specs=in_specs,
        out_specs=VM,
        out_shape=out_shape,
        scratch_shapes=scratch,
        compiler_params=pltpu.CompilerParams(vmem_limit_bytes=8 << 20),
        cost_estimate=pl.CostEstimate(
            flops=2 * taps * PIX * CH * CH, bytes_accessed=4 * PIX * CH, transcendentals=PIX * CH
        ),
        name=name,
    )


def section(e, first, middle, second, core, which):
    one = call(functools.partial(first_kernel, which), [VM] * 2, FRAME_OUT, [WIDE], 9, "conv_first")
    a_outer = one(e[0], first)
    cross = sent(a_outer, outward)
    a_inner = one(e[1], first)
    near = sent(a_inner, other_core)
    out = []
    for role, (own, other, beyond) in enumerate(((a_outer, a_inner, cross), (a_inner, a_outer, near))):
        two = functools.partial(second_kernel, which, role)
        acc = call(two, [SM] + [VM] * 4, FRAME_SUM, [WIDE], 11, "conv_second")(core, own, other, middle, second)
        last = functools.partial(last_kernel, which, role)
        out.append(call(last, [SM] + [VM] * 4, FRAME_OUT, [], 1, "halo_and_residual")(core, acc, e[role], beyond, second))
    return tuple(out)


def joined(h, skip):
    return tuple(((a.astype(F32) + b.astype(F32)) * skip_scale).astype(BF16) for a, b in zip(h, skip))


def hop(frames, source, target):
    return tuple(sent(f, plane_to_plane(source, target)) for f in frames)


def spread_clips(noisy):
    zlo, core, x = (lax.axis_index(n) for n in ("zlo", "core", "x"))
    clips = noisy.reshape(4, PIX, CH)
    got = []
    for r in range(2):
        clip = lax.dynamic_index_in_dim(clips, 2 * zlo + (r ^ core), 0, keepdims=False)

        def route(sx, sy, sz, sc, r=r):
            hi, lo = sz // 2, sz % 2
            clip = 2 * lo + (r ^ sc)
            return (clip, sy, (2 * sx + hi // 2 - 2 * clip) % NZ, hi % 2) if sy == NY - 1 else None

        got.append(sent(clip, route))
    even = (x ^ core) % 2 == 0
    frames = jnp.where(even, got[0], got[1]), jnp.where(even, got[1], got[0])
    frames = jnp.stack(frames)
    return frames, sent(frames, plane_to_plane(NY - 1, 0))


def deliver(h):
    y, zlo, core, x = (lax.axis_index(n) for n in ("y", "zlo", "core", "x"))
    rows = jnp.stack(h).reshape(2, NY, 2, 2, SIDE, CH)
    mine = rows[:, NY - 1]
    for target in range(NY - 1):
        got = sent(rows[:, target], plane_to_plane(NY - 1, target))
        mine = jnp.where(y == target, got, mine)
    natural = jnp.where(core == 0, mine, mine[::-1])
    got = []
    for r in range(2):

        def to_owner(sx, sy, sz, sc, r=r):
            block = block_of(sx, sz)
            return (block // 2, sy, 2 * (2 * (block % 2) + sc) + (sx ^ r) % 2, sx // 2)

        message = lax.dynamic_index_in_dim(natural, (x ^ r) % 2, 1, keepdims=False)
        got.append(sent(message, to_owner))
    pair = jnp.stack([jnp.where(zlo == 0, got[0], got[1]), jnp.where(zlo == 0, got[1], got[0])])
    kept = lax.dynamic_index_in_dim(pair, core, 1, keepdims=False)
    swapped = sent(lax.dynamic_index_in_dim(pair, 1 - core, 1, keepdims=False), other_core)
    out = jnp.stack([jnp.where(core == 0, kept, swapped), jnp.where(core == 0, swapped, kept)])
    return out.reshape(4, 1, 2, SIDE, CH)


def put(buffer, piece, *start):
    return lax.dynamic_update_slice(buffer, piece, start)


def gathered(conv_first, conv_second, temporal):
    conv_first = jnp.concatenate([conv_first, temporal[1:2]], axis=0)
    x, zhi, zlo, core = (lax.axis_index(n).astype(jnp.uint32) for n in ("x", "zhi", "zlo", "core"))
    z = 2 * zhi + zlo
    zero = jnp.uint32(0)

    tail = jnp.concatenate([conv_second, temporal[0:1], temporal[2:3]], axis=0)
    taps = tail.shape[0]
    by_z = [(tail, 0)]
    right = left = tail
    for d in range(1, 5):
        right = sent(right, along(0, 1))
        if d == 2:
            right, conv_first = lax.optimization_barrier((right, conv_first))
        by_z.append((right, -d))
        if d < 4:
            left = sent(left, along(0, -1))
            by_z.append((left, d))
    tails = jnp.zeros((taps, 2, NZ // 2, 16, CH), BF16)
    for piece, offset in by_z:
        source = (z + np.uint32(offset % NZ)) & np.uint32(NZ - 1)
        tails = put(tails, piece.reshape(taps, 1, 1, 16, CH), zero, source & 1, source >> 1, zero, zero)
    x_right = sent(conv_first, along(1, 0))
    x_left = sent(conv_first, along(-1, 0))
    far = sent(x_right, along(1, 0))
    row = jnp.zeros((10, NX, 16, CH), BF16)
    for piece, offset in ((conv_first, 0), (x_right, -1), (x_left, 1), (far, 2)):
        row = put(row, piece.reshape(10, 1, 16, CH), zero, (x + np.uint32(offset % NX)) & np.uint32(NX - 1), zero, zero)

    tails, row = lax.optimization_barrier((tails, row))
    second = lax.all_gather(tails, ("x", "core"), axis=0, tiled=False)
    second = second.reshape(NX, 2, taps, 2, NZ // 2, 16, CH)

    pieces = [(row, 0, 0)]
    right = left = row
    for d in range(1, 4):
        right, left = sent(right, along(0, 1)), sent(left, along(0, -1))
        pieces += [(right, -d, 0), (left, d, 0)]
    half = NX // 2
    pieces.append((sent(right[:, :half], along(0, 1)), 4, 0))
    pieces.append((sent(left[:, half:], along(0, -1)), 4, half))
    first = jnp.zeros((10, 2, NX, NZ // 2, 2, 16, CH), BF16)
    for piece, offset, start in pieces:
        source = (z + np.uint32(offset % NZ)) & np.uint32(NZ - 1)
        for block, owner in ((piece, core), (sent(piece, other_core), core ^ 1)):
            block = block.reshape(10, 1, -1, 1, 1, 16, CH)
            at = (zero, source & 1, jnp.uint32(start), source >> 1, owner, zero, zero)
            first = put(first, block, *at)
    return first.reshape(10, 2 * CH, CH), second


def on_device(noisy, conv_first, conv_second, temporal):
    frames, passed = spread_clips(noisy)
    first, second = gathered(conv_first[0], conv_second[0], temporal[0])
    first, frames, passed = lax.optimization_barrier((first, frames, passed))
    e0 = jnp.where(lax.axis_index("y") == 0, passed, frames)
    e0 = e0[0], e0[1]
    middle = first[9]
    core = lax.axis_index("core").astype(jnp.int32).reshape(1)

    def run(e, which):
        return section(e, first, middle, second, core, which)

    e1 = run(e0, 0)
    skip6 = hop(e1, 0, 3)
    e2 = hop(run(e1, 1), 0, 1)
    skip5 = hop(e2, 1, 2)
    e3 = run(e2, 0)
    e4 = hop(joined(run(e3, 1), e3), 1, 2)
    h = run(e4, 0)
    h = hop(run(joined(h, skip5), 1), 2, 3)
    h = run(joined(h, skip6), 0)
    h = run(joined(h, e0), 1)
    return deliver(h)


def solution(mesh):
    fine = Mesh(mesh.devices.reshape(NY, 2, NX, NZ // 2, 2), AXES)
    weight_spec = P(SEGMENT, None, FRAME, None)
    return jax.shard_map(
        on_device,
        mesh=fine,
        in_specs=(P(None, FRAME), weight_spec, weight_spec, weight_spec),
        out_specs=P(None, FRAME, SEGMENT),
        check_vma=False,
    )
```
